32 devices in a mesh: gx: 8 (over z, core), gy: 4 (over y, x).
Axes of the slice: x: 2, y: 2, z: 4, core: 2. Of those that a mesh axis runs over, the one named last changes fastest.
Arguments:
- tokens: bfloat16 [64, 32, 8, 768], P('gx', 'gy'), may hold values from -64 to 64
- target: bfloat16 [64, 32, 8, 768], P('gx', 'gy'), may hold values from -4 to 4
- norm_gain: float32 [768], replicated, may hold values from 0.1 to 1.9
- qkv_weight: bfloat16 [768, 1152], P('gy'), may hold values from -4 to 4
- proj_weight: bfloat16 [384, 768], P('gy'), may hold values from -1.5 to 1.5
Outputs:
- block_out: bfloat16 [64, 32, 8, 768], P('gx', 'gy')
- qkv_grad: float32 [768, 1152], P('gy')
The draws below stay inside these ranges and needn't reach their ends.
All inputs are finite; a program needn't handle non-finite values.
Results may differ from the reference program's by a relative error of at most 0.0094.
Values may be sent and summed in bfloat16 or wider, within the bound.
A program may use at most 64 MiB of HBM per device.

```python
import math
import jax
import jax.numpy as jnp
from jax import lax

D = 768
HEADS = 12
HD = 32
WIN = 8
INNER = 384
NX = 64
NY = 32
NZ = 8
TOKENS = 16384


def draw_tokens(key, part):
    base = jax.random.truncated_normal(key, -6.0, 6.0, (NX, NY, NZ, D), jnp.float32)
    return base.astype(jnp.bfloat16)


def draw_qkv_weight(key, part):
    weights = jax.random.truncated_normal(key, -6.0, 6.0, (D, 3 * INNER), jnp.float32) / jnp.sqrt(jnp.float32(D))
    return weights.astype(jnp.bfloat16)


def levels(rng, extent, pieces, low, high):
    def one(dim, shards_of):
        heights = jax.random.uniform(jax.random.fold_in(jax.random.fold_in(rng, 6), dim), (shards_of,), jnp.float32, low / len(pieces), high / len(pieces))
        return jnp.repeat(jnp.exp(heights), extent[dim] // shards_of).reshape((-1,) + (1,) * (len(extent) - dim - 1))

    level = one(*pieces[0])
    for cut in pieces[1:]:
        level = level * one(*cut)
    return level


def bell_draw(rng, extent, width, bound, pieces=(), held_as=jnp.bfloat16):
    gain = levels(rng, extent, pieces, -0.22, 0.18) if pieces else 1.0
    values = jax.random.normal(rng, extent, jnp.float32) * width * gain
    return jnp.minimum(jnp.maximum(values, -bound), bound).astype(held_as)


def setup_inputs(seed: int = 0) -> dict:
    splits = jax.random.split(jax.random.key(seed), 6)
    tokens = draw_tokens(jax.random.fold_in(splits[5], 71), 0)
    target = bell_draw(splits[1], (NX, NY, NZ, D), 0.5, 4.0, ((0, 8), (1, 4)))
    norm_gain = jnp.clip(1.0 + 0.18 * jax.random.normal(splits[2], (D,), jnp.float32), 0.1, 1.9)
    qkv_weight = draw_qkv_weight(jax.random.fold_in(splits[5], 71), 0)
    proj_weight = bell_draw(splits[4], (INNER, D), 16 ** -0.5, 1.5, ((0, 4),))
    return dict(tokens=tokens, target=target, norm_gain=norm_gain, qkv_weight=qkv_weight, proj_weight=proj_weight)


def narrow(values):
    return lax.optimization_barrier(values.astype(jnp.bfloat16)).astype(jnp.float32)

def layer_norm(tokens, norm_gain):
    widened = tokens.astype(jnp.float32)
    token_mean = lax.optimization_barrier(jnp.mean(widened, -1, keepdims=True))
    centred = widened - token_mean
    variance = lax.optimization_barrier(jnp.mean(centred * centred, -1, keepdims=True))
    return (centred * lax.rsqrt(variance + 1e-05) * norm_gain.astype(jnp.float32)).astype(jnp.bfloat16)

def into_windows(volume):
    ext_x, ext_y, ext_z, channels = volume.shape
    blocks = volume.reshape(ext_x // WIN, WIN, ext_y // WIN, WIN, ext_z // WIN, WIN, channels)
    return blocks.transpose(0, 2, 4, 1, 3, 5, 6).reshape(-1, WIN ** 3, channels)

def from_windows(windows, ext_x, ext_y, ext_z):
    channels = windows.shape[-1]
    blocks = windows.reshape(ext_x // WIN, ext_y // WIN, ext_z // WIN, WIN, WIN, WIN, channels)
    return blocks.transpose(0, 3, 1, 4, 2, 5, 6).reshape(ext_x, ext_y, ext_z, channels)

def split_heads(block):
    return block.astype(jnp.float32).reshape(block.shape[0], HEADS, HD)

def attention_probs(qkv_block):
    queries = split_heads(qkv_block[:, :INNER])
    keys_in = split_heads(qkv_block[:, INNER:2 * INNER])
    values = split_heads(qkv_block[:, 2 * INNER:])
    scores = jnp.einsum('qhd,khd->hqk', queries, keys_in) * HD ** (-0.5)
    row_max = lax.optimization_barrier(jnp.max(scores, -1, keepdims=True))
    exponent = jnp.exp(scores - row_max)
    probs = exponent / lax.optimization_barrier(jnp.sum(exponent, -1, keepdims=True))
    return (probs, queries, keys_in, values)

def window_forward(qkv_block):
    probs, queries, keys_in, values = attention_probs(qkv_block)
    mixed = jnp.einsum('hqk,khd->qhd', narrow(probs), values)
    return mixed.reshape(-1, INNER).astype(jnp.bfloat16)

def window_backward(inputs_pair):
    qkv_block, grad_block = inputs_pair
    probs, queries, keys_in, values = attention_probs(qkv_block)
    grad_mixed = split_heads(grad_block)
    grad_probs = jnp.einsum('qhd,khd->hqk', grad_mixed, values)
    grad_values = jnp.einsum('hqk,qhd->khd', narrow(probs), grad_mixed).astype(jnp.bfloat16)
    row_dot = lax.optimization_barrier(jnp.sum(grad_probs * probs, -1, keepdims=True))
    grad_scores = narrow(probs * (grad_probs - row_dot))
    grad_queries = (jnp.einsum('hqk,khd->qhd', grad_scores, keys_in) * HD ** (-0.5)).astype(jnp.bfloat16)
    grad_keys = (jnp.einsum('hqk,qhd->khd', grad_scores, queries) * HD ** (-0.5)).astype(jnp.bfloat16)
    return jnp.concatenate([grad_queries.reshape(-1, INNER), grad_keys.reshape(-1, INNER), grad_values.reshape(-1, INNER)], 1)

def reference(tokens, target, norm_gain, qkv_weight, proj_weight):
    half_width = WIN // 2
    normed = layer_norm(tokens, norm_gain)
    shifted = jnp.roll(normed, (-half_width, -half_width, -half_width), axis=(0, 1, 2))
    windows_in = into_windows(shifted)
    flat_in = windows_in.reshape(-1, D)
    qkv_act = jnp.dot(flat_in, qkv_weight, preferred_element_type=jnp.float32).astype(jnp.bfloat16)
    qkv_act = qkv_act.reshape(windows_in.shape[0], WIN ** 3, 3 * INNER)
    attn_out = lax.map(window_forward, qkv_act)
    block_shift = jnp.dot(attn_out.reshape(-1, INNER), proj_weight, preferred_element_type=jnp.float32).astype(jnp.bfloat16)
    block_vol = from_windows(block_shift.reshape(-1, WIN ** 3, D), NX, NY, NZ)
    block_out = jnp.roll(block_vol, (half_width, half_width, half_width), axis=(0, 1, 2))
    grad_out = ((block_out.astype(jnp.float32) - target.astype(jnp.float32)) * (2.0 / math.sqrt(TOKENS))).astype(jnp.bfloat16)
    grad_shift = into_windows(jnp.roll(grad_out, (-half_width, -half_width, -half_width), axis=(0, 1, 2)))
    grad_attn = jnp.dot(grad_shift.reshape(-1, D), proj_weight.T, preferred_element_type=jnp.float32).astype(jnp.bfloat16)
    grad_qkv = lax.map(window_backward, (qkv_act, grad_attn.reshape(-1, WIN ** 3, INNER)))
    qkv_grad = jnp.dot(flat_in.T, grad_qkv.reshape(-1, 3 * INNER), preferred_element_type=jnp.float32)
    return (block_out, qkv_grad)
```

```python
import functools
import math

import jax
import jax.numpy as jnp
from jax import lax
from jax.experimental import pallas as pl
from jax.experimental.pallas import tpu as pltpu
from jax.sharding import PartitionSpec as P

HEADS = 12
HD = 32
WIN = 8
HALF = WIN // 2
INNER = HEADS * HD
FG = 3
FH = HEADS // FG
FC = FH * HD
GROUPS = (
    ((0, 0, 4), (1, 0, 4), (2, 0, 4)),
    ((0, 4, 4), (1, 4, 4), (2, 4, 4)),
    ((0, 8, 2), (1, 8, 2), (2, 8, 4)),
    ((0, 10, 2), (1, 10, 2)),
)
SPREAD = (True, True, False, False)
F32 = jnp.float32
BF16 = jnp.bfloat16
MESH = pl.DeviceIdType.MESH
norm_eps = 1e-05


def dot(a, b, ca, cb):
    return lax.dot_general(a, b, (((ca,), (cb,)), ((), ())), preferred_element_type=F32)


def flat_rows(x):
    rows = math.prod(x.shape[:-1])
    if x.shape[-2] % 16 == 0:
        return x.reshape(rows, x.shape[-1])
    return x.astype(F32).reshape(rows, x.shape[-1]).astype(BF16)


def width(group):
    return sum(n for _, _, n in group) * HD


def kernel(nx, ny, spread, wsplit, psplit, loss_scale, tok, tgt, gain, wq, wp, out, grad, *scratch):
    (win, thome, tph, tpw, aw, ah, wbuf, pbuf, projb, xt, qkvt, ebuf, rinv, ot, dot_t, dgrp, outv) = scratch[:17]
    ng = len(GROUPS)
    bufs = [scratch[17 + 7 * i:24 + 7 * i] for i in range(ng)]
    ssem, rsem, lsem = scratch[17 + 7 * ng:]
    nz = nx // 2
    x = lax.axis_index("gx")
    y = lax.axis_index("gy")
    core = lax.rem(x, 2)
    sib = x + 1 - 2 * core
    z = x // 2
    zodd = lax.rem(z, 2)
    zmate = x + 2 - 4 * zodd
    zpair = wsplit == 4
    whalf = wsplit // 2
    ppart = core if psplit == 2 else 0
    counter = [0]

    def gxi(d):
        return lax.rem(x + d + nx, nx)

    def gyi(d):
        return lax.rem(y + d + ny, ny)

    def remote(src, dst, dev):
        k = counter[0]
        counter[0] += 1
        return pltpu.make_async_remote_copy(
            src_ref=src, dst_ref=dst, send_sem=ssem.at[k], recv_sem=rsem.at[k],
            device_id=dev, device_id_type=MESH,
        )

    sent = []

    def go(copies):
        for c in copies:
            c.start()
            sent.append(c)

    peers = [(x, gyi(d)) for d in range(1, ny)]
    peers += [(gxi(1), y), (gxi(-1), y)]
    peers += [(gxi(2 * d), y) for d in range(1, nz)]
    peers += [(gxi(1), gyi(1)), (gxi(-1), gyi(-1))]
    barrier = pltpu.get_barrier_semaphore()
    for dev in peers:
        pl.semaphore_signal(barrier, inc=1, device_id=dev, device_id_type=MESH)
    lcount = [0]

    def local(src, dst):
        k = lcount[0]
        lcount[0] += 1
        c = pltpu.make_async_copy(src, dst, lsem.at[k])
        c.start()
        return c

    w_own = [
        [
            local(
                wq.at[:, :, pl.ds(part * INNER + g * FC, FC)],
                wbuf.at[g, y, :, :, pl.ds(part * FC, FC)],
            )
            for part in range(3)
        ]
        for g in range(FG)
    ]
    zc, pcols = pbuf.shape[2], pbuf.shape[4]
    p_own = [local(wp.at[:, :, pl.ds(k * pcols, pcols)], pbuf.at[y, :, k]) for k in range(zc)]
    own_tok = local(tok.at[pl.ds(HALF, HALF), 1], win.at[0])
    own_tgt = local(tgt, thome)
    for c in w_own[0] + p_own:
        c.wait()
    pl.semaphore_wait(barrier, len(peers))

    quarters = [(0, 1), (1, 0), (1, 1)]

    def w_piece(g, yy, mine=None):
        if g == 0 and zpair:
            return wbuf.at[g, yy, 2 * core + (zodd if mine else 1 - zodd)]
        return wbuf.at[g, yy, pl.ds(core * whalf, whalf)]

    def p_piece(yy, mine):
        if zpair:
            return pbuf.at[yy, ppart, zodd if mine else 1 - zodd]
        return pbuf.at[yy, ppart, 0]

    def spread_y(piece):
        return [remote(piece, piece, (x, gyi(d))) for d in range(1, ny)]

    tok_copies = [
        remote(tok.at[pl.ds(HALF * (1 - a), HALF), 1 - b], win.at[2 * a + b], (gxi(-a), gyi(-b)))
        for a, b in quarters
    ]
    w_copies = [spread_y(w_piece(0, y, True))]
    go(w_copies[0])
    go(tok_copies[1:2])
    p_copies = spread_y(p_piece(y, True))
    go(p_copies)
    go([tok_copies[0], tok_copies[2]])
    for g in range(1, FG):
        for c in w_own[g]:
            c.wait()
        w_copies.append(spread_y(w_piece(g, y)))
        go(w_copies[g])

    def norm(q):
        v = win[q].reshape(-1, win.shape[-1]).astype(F32)
        mean = jnp.mean(v, -1, keepdims=True)
        cen = v - mean
        var = jnp.mean(cen * cen, -1, keepdims=True)
        nrm = cen * lax.rsqrt(var + norm_eps) * gain[...].reshape(1, -1)
        rows = v.shape[0]
        xt[:, q * rows:(q + 1) * rows] = nrm.T.astype(BF16)

    def pass_on(copies, piece, dev):
        onward = []
        for d in range(1, ny):
            copies[d - 1].wait_recv()
            part = piece(gyi(-d))
            onward.append([remote(part, part, to) for to in dev])
            go(onward[-1])
        return [list(c) for c in zip(*onward)]

    own_tok.wait()
    norm(0)
    both = [(zmate, y), (sib, y)] if zpair else [(sib, y)]
    w0 = pass_on(w_copies[0], lambda yy: w_piece(0, yy, True), both)
    tok_copies[1].wait_recv()
    norm(2)
    if zpair:
        p0 = pass_on(p_copies, lambda yy: p_piece(yy, True), both)
        w0 += pass_on(w0[0], lambda yy: w_piece(0, yy, False), [(sib, y)])
        p0 += pass_on(p0[0], lambda yy: p_piece(yy, False), [(sib, y)])
        w0, p0 = w0[1:], p0[1:]
    elif psplit == 2:
        p0 = pass_on(p_copies, lambda yy: p_piece(yy, True), both)
    else:
        p0 = [p_copies]
    for c in sum(p0, []):
        c.wait_recv()
    for k in range(zc):
        projb[:, k * pcols:(k + 1) * pcols] = flat_rows(pbuf[:, :, k])
    own_tgt.wait()
    n_tok = xt.shape[1]
    tph[...] = dot(thome[...].reshape(n_tok, -1), projb[...], 1, 1).astype(BF16).reshape(tph.shape)
    t_copies = [
        remote(tph.at[pl.ds(HALF * (1 - a), HALF), 1 - b], tpw.at[2 * a + b], (gxi(-a), gyi(-b)))
        for a, b in quarters
    ]
    go(t_copies)
    own_t = local(tph.at[pl.ds(HALF, HALF), 1], tpw.at[0])
    for c in sum(w0, []):
        c.wait_recv()
    tok_copies[0].wait_recv()
    norm(1)
    early = n_tok // 4 * 3
    gw3 = 3 * FC

    def qkv(g, lo, hi):
        res = dot(flat_rows(wbuf[g]), xt[:, lo:hi], 0, 0)
        qkvt[g * gw3:(g + 1) * gw3, lo:hi] = res.astype(BF16)

    qkv(0, 0, early)
    tok_copies[2].wait_recv()
    norm(3)
    qkv(0, early, n_tok)

    scale = HD ** (-0.5)
    c2 = scale * math.log2(math.e)

    def rows_of(h, base=0):
        return pl.ds(pl.multiple_of(base + h * HD, HD), HD)

    def load_qkv(part, g, t):
        return qkvt[rows_of(t, g * gw3 + part * FC), :]

    def fwd(g, lo, hi):
        def body(t, carry):
            q, k, v = [load_qkv(part, g, t) for part in range(3)]
            h = g * FH + t
            s = dot(k, q, 0, 0)
            m = jnp.max(s, 0, keepdims=True)
            e = jnp.exp2((s - m) * c2)
            r = 1.0 / jnp.sum(e, 0, keepdims=True)
            eb = e.astype(BF16)
            ebuf[h] = eb
            rinv[h] = r
            ot[rows_of(h), :] = dot(v, eb, 1, 0) * r
            return carry

        lax.fori_loop(lo, hi, body, 0, unroll=2)

    for g in range(FG):
        fwd(g, 0, FH // 2)
        if g + 1 < FG:
            more = pass_on(w_copies[g + 1], lambda yy: w_piece(g + 1, yy), [(sib, y)])
        fwd(g, FH // 2, FH)
        if g + 1 < FG:
            for c in sum(more, []):
                c.wait_recv()
            qkv(g + 1, 0, n_tok)

    attn = ot[...].T.astype(BF16)
    aw[...] = attn.reshape(aw.shape)
    o_copies = [
        remote(aw.at[2 * a + b], ah.at[pl.ds(HALF * (1 - a), HALF), 1 - b], (gxi(a), gyi(b)))
        for a, b in quarters
    ]
    go(o_copies)
    own_a = local(aw.at[0], ah.at[pl.ds(HALF, HALF), 1])
    res = dot(attn, projb[...], 1, 0).astype(BF16)
    back = dot(res, projb[...], 1, 1)
    for c in t_copies:
        c.wait_recv()
    own_t.wait()
    tw = tpw[...].reshape(n_tok, -1).astype(F32)
    dot_t[...] = ((back - tw) * loss_scale).T.astype(BF16)

    def bwd(h0, n, dq=None, dk=None, dv=None):
        g, t0 = h0 // FH, h0 % FH

        def body(i, carry):
            q, k, v = [load_qkv(part, g, t0 + i) for part in range(3)]
            h = h0 + i
            eb = ebuf[h]
            do = dot_t[rows_of(h), :].astype(F32) * rinv[h]
            dob = do.astype(BF16)
            if dq is not None:
                rd = jnp.sum(do * ot[rows_of(h), :], 0, keepdims=True)
                dp = dot(v, dob, 0, 0)
                ds = (eb.astype(F32) * (dp - rd)).astype(BF16)
                dgrp[rows_of(i, dq), :] = (dot(k, ds, 1, 0) * scale).astype(BF16)
                dgrp[rows_of(i, dk), :] = (dot(q, ds, 1, 1) * scale).astype(BF16)
            if dv is not None:
                dgrp[rows_of(i, dv), :] = dot(dob, eb, 1, 1).astype(BF16)
            return carry

        lax.fori_loop(0, n, body, 0, unroll=2)

    st = {}

    def stage_a(i):
        snd1, rcv1 = bufs[i][:2]
        gw = width(GROUPS[i])
        dw = dot(xt[...], dgrp[:gw, :], 1, 1)
        dw = dw.reshape(ny, 2, snd1.shape[2], gw).astype(BF16)
        for cc in range(2):
            snd1[cc] = dw[:, cc]
        st["a", i] = [remote(snd1.at[1 - core], rcv1, (sib, y))]
        go(st["a", i])

    def stage_b(i):
        snd1, rcv1, s1, rcv2 = bufs[i][:4]
        for c in st["a", i]:
            c.wait_recv()
        s1[...] = (snd1[core].astype(F32) + rcv1[...].astype(F32)).astype(BF16)
        st["b", i] = [remote(s1.at[gyi(d)], rcv2.at[d - 1], (x, gyi(d))) for d in range(1, ny)]
        go(st["b", i])

    def stage_c(i):
        s1, rcv2, snd3, rcv3 = bufs[i][2:6]
        acc = s1[y].astype(F32)
        for d in range(1, ny):
            st["b", i][d - 1].wait_recv()
            acc = acc + rcv2[d - 1].astype(F32)
        snd3[...] = acc.reshape(snd3.shape).astype(BF16)
        copies = []
        for d in range(1, nz):
            piece = lax.rem(z + d, nz) if spread[i] else 0
            copies.append(remote(snd3.at[piece], rcv3.at[d - 1], (gxi(2 * d), y)))
        st["c", i] = copies
        go(copies)

    def stage_d(i):
        snd3, rcv3, fin = bufs[i][4:]
        piece = z if spread[i] else 0
        acc = snd3[piece].astype(F32)
        for d in range(1, nz):
            st["c", i][d - 1].wait_recv()
            acc = acc + rcv3[d - 1].astype(F32)
        fin[core, piece] = acc.astype(BF16)
        st["d", i] = []
        if spread[i]:
            mine = fin.at[core, z]
            st["d", i] = [remote(mine, mine, (gxi(2 * d), y)) for d in range(1, nz)]
            go(st["d", i])

    def stage_e(i):
        fin = bufs[i][6]
        for c in st["d", i]:
            c.wait_recv()
        st["e", i] = [remote(fin.at[core], fin.at[core], (sib, y))]
        go(st["e", i])

    def stage_f(i):
        for c in st["e", i]:
            c.wait_recv()
        res = flat_rows(bufs[i][6][...])
        at = 0
        for part, h0, n in GROUPS[i]:
            lo = part * INNER + h0 * HD
            grad[:, lo:lo + n * HD] = res[:, at:at + n * HD]
            at += n * HD

    bwd(0, 2, 0, FC, 2 * FC)
    bwd(2, 2, 2 * HD, FC + 2 * HD, 2 * FC + 2 * HD)
    stage_a(0)
    bwd(4, 2, 0, FC, 2 * FC)
    stage_b(0)
    bwd(6, 2, 2 * HD, FC + 2 * HD, 2 * FC + 2 * HD)
    stage_a(1)
    bwd(8, 2, 0, 2 * HD, 4 * HD)
    stage_b(1)
    bwd(10, 2, None, None, 6 * HD)
    stage_a(2)
    bwd(10, 2, 0, 2 * HD)
    stage_a(3)
    stage_b(2)
    stage_c(0)
    stage_b(3)
    for c in o_copies:
        c.wait_recv()
    own_a.wait()
    outv[...] = dot(ah[...].reshape(n_tok, -1), projb[...], 1, 0).astype(BF16)
    put = local(outv, out)
    stage_c(1)
    stage_d(0)
    stage_c(2)
    stage_c(3)
    stage_e(0)
    stage_d(1)
    stage_e(1)
    stage_f(0)
    stage_d(2)
    stage_e(2)
    stage_f(1)
    stage_d(3)
    stage_e(3)
    stage_f(2)
    stage_f(3)
    put.wait()
    for c in sent:
        c.wait_send()


def finish(b_in, g_in, b_out, g_out):
    b_out[...] = b_in[...]
    g_out[...] = g_in[...].astype(F32)


def shards(nx, ny, tokens, target, norm_gain, qkv_weight, proj_weight):
    ex, ey, ez, ch = tokens.shape
    rows = HALF * ez
    wr = qkv_weight.shape[0]
    pr = proj_weight.shape[0]
    wsplit = 4 if wr % 64 == 0 else 2
    psplit = 2 if pr % 32 == 0 else 1
    zc = 2 if wsplit == 4 else 1
    hr = wr // 2
    nz = nx // 2
    spread = [hr % (8 * nz) == 0 and on for on in SPREAD]
    n_tok = ex * ey * ez
    inner3 = qkv_weight.shape[1]
    loss_scale = 2.0 / math.sqrt(n_tok * nx * ny)
    ncopies = 9 + (ny - 1) * (2 * FG + 8)
    ncopies += sum(2 + (ny - 1) + (nz - 1) * (2 if on else 1) for on in spread)
    any_spec = pl.BlockSpec(memory_space=pl.ANY)
    vm_spec = pl.BlockSpec(memory_space=pltpu.VMEM)
    group_bufs = []
    for group, on in zip(GROUPS, spread):
        gw = width(group)
        pieces = nz if on else 1
        prow = hr // pieces
        group_bufs += [
            pltpu.VMEM((2, ny, hr, gw), BF16),
            pltpu.VMEM((ny, hr, gw), BF16),
            pltpu.VMEM((ny, hr, gw), BF16),
            pltpu.VMEM((ny - 1, hr, gw), BF16),
            pltpu.VMEM((pieces, prow, gw), BF16),
            pltpu.VMEM((nz - 1, prow, gw), BF16),
            pltpu.VMEM((2, pieces, prow, gw), BF16),
        ]
    block, grad = pl.pallas_call(
        functools.partial(kernel, nx, ny, spread, wsplit, psplit, loss_scale),
        out_shape=(
            jax.ShapeDtypeStruct((n_tok, ch), BF16),
            jax.ShapeDtypeStruct((wr, inner3), BF16),
        ),
        in_specs=[any_spec, any_spec, vm_spec, any_spec, any_spec],
        out_specs=(any_spec, vm_spec),
        scratch_shapes=[
            pltpu.VMEM((4, HALF, rows, ch), BF16),
            pltpu.VMEM((ex, 2, rows, ch), BF16),
            pltpu.VMEM((ex, 2, rows, INNER), BF16),
            pltpu.VMEM((4, HALF, rows, INNER), BF16),
            pltpu.VMEM((4, HALF, rows, INNER), BF16),
            pltpu.VMEM((ex, 2, rows, INNER), BF16),
            pltpu.VMEM((FG, ny, wsplit, wr // wsplit, 3 * FC), BF16),
            pltpu.VMEM((ny, psplit, zc, pr // psplit, ch // zc), BF16),
            pltpu.VMEM((INNER, ch), BF16),
            pltpu.VMEM((ch, n_tok), BF16),
            pltpu.VMEM((inner3, n_tok), BF16),
            pltpu.VMEM((HEADS, n_tok, n_tok), BF16),
            pltpu.VMEM((HEADS, 1, n_tok), F32),
            pltpu.VMEM((INNER, n_tok), F32),
            pltpu.VMEM((INNER, n_tok), BF16),
            pltpu.VMEM((3 * FC, n_tok), BF16),
            pltpu.VMEM((n_tok, ch), BF16),
            *group_bufs,
            pltpu.SemaphoreType.DMA((ncopies,)),
            pltpu.SemaphoreType.DMA((ncopies,)),
            pltpu.SemaphoreType.DMA((3 * FG + 7,)),
        ],
        compiler_params=pltpu.CompilerParams(
            collective_id=0, has_side_effects=True, vmem_limit_bytes=60 * 2**20
        ),
        name="step",
    )(
        tokens.reshape(ex, 2, rows, ch),
        target.reshape(ex, 2, rows, ch),
        norm_gain,
        qkv_weight.reshape(wsplit, wr // wsplit, inner3),
        proj_weight.reshape(psplit, pr // psplit, ch),
    )
    steps = 4 if wr % 64 == 0 else 1
    bspec = pl.BlockSpec((n_tok // steps, ch), lambda i: (i, 0))
    gspec = pl.BlockSpec((wr // steps, inner3), lambda i: (i, 0))
    block, grad = pl.pallas_call(
        finish,
        grid=(steps,),
        out_shape=(
            jax.ShapeDtypeStruct(block.shape, BF16),
            jax.ShapeDtypeStruct(grad.shape, F32),
        ),
        in_specs=[bspec, gspec],
        out_specs=(bspec, gspec),
        name="finish",
    )(block, grad)
    return block.reshape(ex, ey, ez, ch), grad


def solution(mesh):
    nx, ny = mesh.shape["gx"], mesh.shape["gy"]
    in_specs = (
        P("gx", "gy", None, None),
        P("gx", "gy", None, None),
        P(),
        P("gy", None),
        P("gy", None),
    )
    out_specs = (P("gx", "gy", None, None), P("gy", None))
    return jax.shard_map(
        functools.partial(shards, nx, ny),
        mesh=mesh, in_specs=in_specs, out_specs=out_specs, check_vma=False,
    )
```

```python
import functools
import math

import jax
import jax.numpy as jnp
from jax import lax
from jax.experimental import pallas as pl
from jax.experimental.pallas import tpu as pltpu
from jax.sharding import PartitionSpec as P

HEADS = 12
HD = 32
WIN = 8
HALF = WIN // 2
INNER = HEADS * HD
FG = 3
FH = HEADS // FG
FC = FH * HD
GROUPS = (
    ((0, 0, 4), (1, 0, 4), (2, 0, 4)),
    ((0, 4, 4), (1, 4, 4), (2, 4, 4)),
    ((0, 8, 2), (1, 8, 2), (2, 8, 4)),
    ((0, 10, 2), (1, 10, 2)),
)
SPREAD = (True, True, False, False)
F32 = jnp.float32
BF16 = jnp.bfloat16
MESH = pl.DeviceIdType.MESH
norm_eps = 1e-05


def dot(a, b, ca, cb):
    return lax.dot_general(a, b, (((ca,), (cb,)), ((), ())), preferred_element_type=F32)


def flat_rows(x):
    rows = math.prod(x.shape[:-1])
    if x.shape[-2] % 16 == 0:
        return x.reshape(rows, x.shape[-1])
    return x.astype(F32).reshape(rows, x.shape[-1]).astype(BF16)


def width(group):
    return sum(n for _, _, n in group) * HD


def kernel(nx, ny, spread, wsplit, psplit, loss_scale, tok, tgt, gain, wq, wp, out, grad, *scratch):
    (win, thome, tph, tpw, aw, ah, wbuf, pbuf, projb, xt, qkvt, ebuf, rinv, ot, dot_t, dgrp, outv) = scratch[:17]
    ng = len(GROUPS)
    bufs = [scratch[17 + 7 * i:24 + 7 * i] for i in range(ng)]
    ssem, rsem, lsem = scratch[17 + 7 * ng:]
    nz = nx // 2
    x = lax.axis_index("gx")
    y = lax.axis_index("gy")
    core = lax.rem(x, 2)
    sib = x + 1 - 2 * core
    z = x // 2
    zodd = lax.rem(z, 2)
    zmate = x + 2 - 4 * zodd
    zpair = wsplit == 4
    whalf = wsplit // 2
    ppart = core if psplit == 2 else 0
    counter = [0]

    def gxi(d):
        return lax.rem(x + d + nx, nx)

    def gyi(d):
        return lax.rem(y + d + ny, ny)

    def remote(src, dst, dev):
        k = counter[0]
        counter[0] += 1
        return pltpu.make_async_remote_copy(
            src_ref=src, dst_ref=dst, send_sem=ssem.at[k], recv_sem=rsem.at[k],
            device_id=dev, device_id_type=MESH,
        )

    sent = []

    def go(copies):
        for c in copies:
            c.start()
            sent.append(c)

    peers = [(x, gyi(d)) for d in range(1, ny)]
    peers += [(gxi(1), y), (gxi(-1), y)]
    peers += [(gxi(2 * d), y) for d in range(1, nz)]
    side = 1 - 2 * core
    peers += [(gxi(1), gyi(side)), (gxi(-1), gyi(side))]
    barrier = pltpu.get_barrier_semaphore()
    for dev in peers:
        pl.semaphore_signal(barrier, inc=1, device_id=dev, device_id_type=MESH)
    lcount = [0]

    def local(src, dst):
        k = lcount[0]
        lcount[0] += 1
        c = pltpu.make_async_copy(src, dst, lsem.at[k])
        c.start()
        return c

    w_own = [
        [
            local(
                wq.at[:, :, pl.ds(part * INNER + g * FC, FC)],
                wbuf.at[g, y, :, :, pl.ds(part * FC, FC)],
            )
            for part in range(3)
        ]
        for g in range(FG)
    ]
    zc, pcols = pbuf.shape[2], pbuf.shape[4]
    p_own = [local(wp.at[:, :, pl.ds(k * pcols, pcols)], pbuf.at[y, :, k]) for k in range(zc)]
    own_tok = local(tok.at[pl.ds(HALF, HALF), 1 - core], win.at[0])
    own_tgt = local(tgt, thome)
    for c in w_own[0] + p_own:
        c.wait()
    pl.semaphore_wait(barrier, len(peers))

    quarters = [(0, 1), (1, 0), (1, 1)]

    def to_windows(home, wins):
        copies = []
        for a, b in quarters:
            host = 1 - core if a else core
            src = home.at[pl.ds(HALF * (1 - a), HALF), host if b else 1 - host]
            dev = (gxi(-a), gyi(2 * host - 1) if b else y)
            copies.append(remote(src, wins.at[2 * a + b], dev))
        return copies

    relay = ny == 4 and zpair and psplit == 2
    items = (0, FG, *range(1, FG))

    def piece(it, yy, mine):
        if it == FG:
            if zpair:
                return pbuf.at[yy, ppart, zodd if mine else 1 - zodd]
            return pbuf.at[yy, ppart, 0]
        if zpair:
            return wbuf.at[it, yy, 2 * core + (zodd if mine else 1 - zodd)]
        return wbuf.at[it, yy, pl.ds(core * whalf, whalf)]

    def send(it, yy, mine, dev):
        part = piece(it, yy, mine)
        c = remote(part, part, dev)
        go([c])
        return c

    y1 = y + 1 - 2 * lax.rem(y, 2)
    y2 = gyi(2)
    y3 = ny - 1 - y
    tok_copies = to_windows(tok, win)
    hop = {}
    near = [gyi(d) for d in range(1, ny)]
    go(tok_copies[1:2])
    if relay:
        for it in items:
            if it not in (0, FG):
                for c in w_own[it]:
                    c.wait()
            hop["x", it] = send(it, y, True, (x, y1))
            hop["y", it] = send(it, y, True, (x, y2))
        go([tok_copies[0], tok_copies[2]])
    else:
        for it in items:
            if it not in (0, FG):
                for c in w_own[it]:
                    c.wait()
            if it == 1:
                go([tok_copies[0], tok_copies[2]])
            hop["y", it] = [send(it, y, True, (x, dev)) for dev in near]

    def norm(q):
        v = win[q].reshape(-1, win.shape[-1]).astype(F32)
        mean = jnp.mean(v, -1, keepdims=True)
        cen = v - mean
        var = jnp.mean(cen * cen, -1, keepdims=True)
        nrm = cen * lax.rsqrt(var + norm_eps) * gain[...].reshape(1, -1)
        rows = v.shape[0]
        xt[:, q * rows:(q + 1) * rows] = nrm.T.astype(BF16)

    landed = {it: [] for it in items}

    def onward(it, yy, zsend=True):
        if zsend:
            hop["z", it] = hop.get(("z", it), []) + [(yy, send(it, yy, True, (zmate, y)))]
        landed[it].append(send(it, yy, True, (sib, y)))

    def first_hops(it, zsend):
        hop["x", it].wait_recv()
        hop["d", it] = send(it, y1, True, (x, y2))
        onward(it, y1, zsend)
        hop["y", it].wait_recv()
        onward(it, y2, zsend)

    def last_hops(it):
        for yy, c in hop["z", it]:
            c.wait_recv()
            landed[it].append(send(it, yy, False, (sib, y)))

    def settle(it):
        for c in landed[it]:
            c.wait_recv()

    own_tok.wait()
    norm(0)
    if relay:
        for it in (0, FG):
            first_hops(it, True)
        for it in range(1, FG):
            first_hops(it, False)
        tok_copies[1].wait_recv()
        norm(2)
        for it in (0, FG):
            hop["d", it].wait_recv()
            onward(it, y3)
        for it in range(1, FG):
            hop["z", it] = [(yy, send(it, yy, True, (zmate, y))) for yy in (y1, y2)]
            hop["d", it].wait_recv()
            onward(it, y3)
        tok_copies[0].wait_recv()
        norm(1)
        for it in (0, FG):
            last_hops(it)
        tok_copies[2].wait_recv()
        norm(3)
    else:
        for it in (0, FG):
            for d in range(1, ny):
                hop["y", it][d - 1].wait_recv()
                if it < FG or psplit == 2:
                    landed[it].append(send(it, gyi(-d), True, (sib, y)))
        for t in (1, 0, 2):
            tok_copies[t].wait_recv()
            norm(quarters[t][0] * 2 + quarters[t][1])

    def late(it):
        if relay:
            last_hops(it)
        else:
            for d in range(1, ny):
                hop["y", it][d - 1].wait_recv()
                landed[it].append(send(it, gyi(-d), True, (sib, y)))

    settle(FG)
    for k in range(zc):
        projb[:, k * pcols:(k + 1) * pcols] = flat_rows(pbuf[:, :, k])
    own_tgt.wait()
    n_tok = xt.shape[1]
    tph[...] = dot(thome[...].reshape(n_tok, -1), projb[...], 1, 1).astype(BF16).reshape(tph.shape)
    t_copies = to_windows(tph, tpw)
    go(t_copies)
    own_t = local(tph.at[pl.ds(HALF, HALF), 1 - core], tpw.at[0])
    gw3 = 3 * FC

    def qkv(g):
        settle(g)
        qkvt[g * gw3:(g + 1) * gw3, :] = dot(flat_rows(wbuf[g]), xt[...], 0, 0).astype(BF16)

    qkv(0)

    scale = HD ** (-0.5)
    c2 = scale * math.log2(math.e)

    def rows_of(h, base=0):
        return pl.ds(pl.multiple_of(base + h * HD, HD), HD)

    def load_qkv(part, g, t):
        return qkvt[rows_of(t, g * gw3 + part * FC), :]

    def fwd(g, lo, hi):
        def body(t, carry):
            q, k, v = [load_qkv(part, g, t) for part in range(3)]
            h = g * FH + t
            s = dot(k, q, 0, 0)
            m = jnp.max(s, 0, keepdims=True)
            e = jnp.exp2((s - m) * c2)
            r = 1.0 / jnp.sum(e, 0, keepdims=True)
            eb = e.astype(BF16)
            ebuf[h] = eb
            rinv[h] = r
            ot[rows_of(h), :] = dot(v, eb, 1, 0) * r
            return carry

        lax.fori_loop(lo, hi, body, 0, unroll=2)

    for g in range(FG):
        fwd(g, 0, FH // 2)
        if g + 1 < FG:
            late(g + 1)
        fwd(g, FH // 2, FH)
        if g + 1 < FG:
            qkv(g + 1)

    attn = ot[...].T.astype(BF16)
    aw[...] = attn.reshape(aw.shape)
    o_copies = [
        remote(
            aw.at[2 * a + b],
            ah.at[pl.ds(HALF * (1 - a), HALF), core if b else 1 - core],
            (gxi(a), gyi(side) if b else y),
        )
        for a, b in quarters
    ]
    go(o_copies)
    own_a = local(aw.at[0], ah.at[pl.ds(HALF, HALF), 1 - core])
    res = dot(attn, projb[...], 1, 0).astype(BF16)
    back = dot(res, projb[...], 1, 1)
    for c in t_copies:
        c.wait_recv()
    own_t.wait()
    tw = tpw[...].reshape(n_tok, -1).astype(F32)
    dot_t[...] = ((back - tw) * loss_scale).T.astype(BF16)

    def bwd(h0, n, dq=None, dk=None, dv=None):
        g, t0 = h0 // FH, h0 % FH

        def body(i, carry):
            q, k, v = [load_qkv(part, g, t0 + i) for part in range(3)]
            h = h0 + i
            eb = ebuf[h]
            do = dot_t[rows_of(h), :].astype(F32) * rinv[h]
            dob = do.astype(BF16)
            if dq is not None:
                rd = jnp.sum(do * ot[rows_of(h), :], 0, keepdims=True)
                dp = dot(v, dob, 0, 0)
                ds = (eb.astype(F32) * (dp - rd)).astype(BF16)
                dgrp[rows_of(i, dq), :] = (dot(k, ds, 1, 0) * scale).astype(BF16)
                dgrp[rows_of(i, dk), :] = (dot(q, ds, 1, 1) * scale).astype(BF16)
            if dv is not None:
                dgrp[rows_of(i, dv), :] = dot(dob, eb, 1, 1).astype(BF16)
            return carry

        lax.fori_loop(0, n, body, 0, unroll=2)

    st = {}

    def stage_a(i):
        snd1, rcv1 = bufs[i][:2]
        gw = width(GROUPS[i])
        dw = dot(xt[...], dgrp[:gw, :], 1, 1)
        dw = dw.reshape(ny, 2, snd1.shape[2], gw).astype(BF16)
        for cc in range(2):
            snd1[cc] = dw[:, cc]
        st["a", i] = [remote(snd1.at[1 - core], rcv1, (sib, y))]
        go(st["a", i])

    def stage_b(i):
        snd1, rcv1, s1, rcv2 = bufs[i][:4]
        for c in st["a", i]:
            c.wait_recv()
        s1[...] = (snd1[core].astype(F32) + rcv1[...].astype(F32)).astype(BF16)
        st["b", i] = [remote(s1.at[gyi(d)], rcv2.at[d - 1], (x, gyi(d))) for d in range(1, ny)]
        go(st["b", i])

    def stage_c(i):
        s1, rcv2, snd3, rcv3 = bufs[i][2:6]
        acc = s1[y].astype(F32)
        for d in range(1, ny):
            st["b", i][d - 1].wait_recv()
            acc = acc + rcv2[d - 1].astype(F32)
        snd3[...] = acc.reshape(snd3.shape).astype(BF16)
        copies = []
        for d in range(1, nz):
            piece = lax.rem(z + d, nz) if spread[i] else 0
            copies.append(remote(snd3.at[piece], rcv3.at[d - 1], (gxi(2 * d), y)))
        st["c", i] = copies
        go(copies)

    def stage_d(i):
        snd3, rcv3, fin = bufs[i][4:]
        piece = z if spread[i] else 0
        acc = snd3[piece].astype(F32)
        for d in range(1, nz):
            st["c", i][d - 1].wait_recv()
            acc = acc + rcv3[d - 1].astype(F32)
        fin[core, piece] = acc.astype(BF16)
        st["d", i] = []
        if spread[i]:
            mine = fin.at[core, z]
            st["d", i] = [remote(mine, mine, (gxi(2 * d), y)) for d in range(1, nz)]
            go(st["d", i])

    def stage_e(i):
        fin = bufs[i][6]
        for c in st["d", i]:
            c.wait_recv()
        st["e", i] = [remote(fin.at[core], fin.at[core], (sib, y))]
        go(st["e", i])

    def stage_f(i):
        for c in st["e", i]:
            c.wait_recv()
        res = flat_rows(bufs[i][6][...])
        at = 0
        for part, h0, n in GROUPS[i]:
            lo = part * INNER + h0 * HD
            grad[:, lo:lo + n * HD] = res[:, at:at + n * HD]
            at += n * HD

    bwd(0, 2, 0, FC, 2 * FC)
    bwd(2, 2, 2 * HD, FC + 2 * HD, 2 * FC + 2 * HD)
    stage_a(0)
    bwd(4, 2, 0, FC, 2 * FC)
    stage_b(0)
    bwd(6, 2, 2 * HD, FC + 2 * HD, 2 * FC + 2 * HD)
    stage_a(1)
    bwd(8, 2, 0, 2 * HD, 4 * HD)
    stage_b(1)
    bwd(10, 2, None, None, 6 * HD)
    stage_a(2)
    bwd(10, 2, 0, 2 * HD)
    stage_a(3)
    stage_b(2)
    stage_c(0)
    stage_b(3)
    for c in o_copies:
        c.wait_recv()
    own_a.wait()
    outv[...] = dot(ah[...].reshape(n_tok, -1), projb[...], 1, 0).astype(BF16)
    put = local(outv, out)
    stage_c(1)
    stage_d(0)
    stage_c(2)
    stage_c(3)
    stage_e(0)
    stage_d(1)
    stage_e(1)
    stage_f(0)
    stage_d(2)
    stage_e(2)
    stage_f(1)
    stage_d(3)
    stage_e(3)
    stage_f(2)
    stage_f(3)
    put.wait()
    for c in sent:
        c.wait_send()


def finish(b_in, g_in, b_out, g_out):
    b_out[...] = b_in[...]
    g_out[...] = g_in[...].astype(F32)


def shards(nx, ny, tokens, target, norm_gain, qkv_weight, proj_weight):
    ex, ey, ez, ch = tokens.shape
    rows = HALF * ez
    wr = qkv_weight.shape[0]
    pr = proj_weight.shape[0]
    wsplit = 4 if wr % 64 == 0 else 2
    psplit = 2 if pr % 32 == 0 else 1
    zc = 2 if wsplit == 4 else 1
    hr = wr // 2
    nz = nx // 2
    spread = [hr % (8 * nz) == 0 and on for on in SPREAD]
    n_tok = ex * ey * ez
    inner3 = qkv_weight.shape[1]
    loss_scale = 2.0 / math.sqrt(n_tok * nx * ny)
    ncopies = 9 + (FG + 1) * max(12, 2 * (ny - 1))
    ncopies += sum(2 + (ny - 1) + (nz - 1) * (2 if on else 1) for on in spread)
    any_spec = pl.BlockSpec(memory_space=pl.ANY)
    vm_spec = pl.BlockSpec(memory_space=pltpu.VMEM)
    group_bufs = []
    for group, on in zip(GROUPS, spread):
        gw = width(group)
        pieces = nz if on else 1
        prow = hr // pieces
        group_bufs += [
            pltpu.VMEM((2, ny, hr, gw), BF16),
            pltpu.VMEM((ny, hr, gw), BF16),
            pltpu.VMEM((ny, hr, gw), BF16),
            pltpu.VMEM((ny - 1, hr, gw), BF16),
            pltpu.VMEM((pieces, prow, gw), BF16),
            pltpu.VMEM((nz - 1, prow, gw), BF16),
            pltpu.VMEM((2, pieces, prow, gw), BF16),
        ]
    block, grad = pl.pallas_call(
        functools.partial(kernel, nx, ny, spread, wsplit, psplit, loss_scale),
        out_shape=(
            jax.ShapeDtypeStruct((n_tok, ch), BF16),
            jax.ShapeDtypeStruct((wr, inner3), BF16),
        ),
        in_specs=[any_spec, any_spec, vm_spec, any_spec, any_spec],
        out_specs=(any_spec, vm_spec),
        scratch_shapes=[
            pltpu.VMEM((4, HALF, rows, ch), BF16),
            pltpu.VMEM((ex, 2, rows, ch), BF16),
            pltpu.VMEM((ex, 2, rows, INNER), BF16),
            pltpu.VMEM((4, HALF, rows, INNER), BF16),
            pltpu.VMEM((4, HALF, rows, INNER), BF16),
            pltpu.VMEM((ex, 2, rows, INNER), BF16),
            pltpu.VMEM((FG, ny, wsplit, wr // wsplit, 3 * FC), BF16),
            pltpu.VMEM((ny, psplit, zc, pr // psplit, ch // zc), BF16),
            pltpu.VMEM((INNER, ch), BF16),
            pltpu.VMEM((ch, n_tok), BF16),
            pltpu.VMEM((inner3, n_tok), BF16),
            pltpu.VMEM((HEADS, n_tok, n_tok), BF16),
            pltpu.VMEM((HEADS, 1, n_tok), F32),
            pltpu.VMEM((INNER, n_tok), F32),
            pltpu.VMEM((INNER, n_tok), BF16),
            pltpu.VMEM((3 * FC, n_tok), BF16),
            pltpu.VMEM((n_tok, ch), BF16),
            *group_bufs,
            pltpu.SemaphoreType.DMA((ncopies,)),
            pltpu.SemaphoreType.DMA((ncopies,)),
            pltpu.SemaphoreType.DMA((3 * FG + 7,)),
        ],
        compiler_params=pltpu.CompilerParams(
            collective_id=0, has_side_effects=True, vmem_limit_bytes=60 * 2**20
        ),
        name="step",
    )(
        tokens.reshape(ex, 2, rows, ch),
        target.reshape(ex, 2, rows, ch),
        norm_gain,
        qkv_weight.reshape(wsplit, wr // wsplit, inner3),
        proj_weight.reshape(psplit, pr // psplit, ch),
    )
    steps = 4 if wr % 64 == 0 else 1
    bspec = pl.BlockSpec((n_tok // steps, ch), lambda i: (i, 0))
    gspec = pl.BlockSpec((wr // steps, inner3), lambda i: (i, 0))
    block, grad = pl.pallas_call(
        finish,
        grid=(steps,),
        out_shape=(
            jax.ShapeDtypeStruct(block.shape, BF16),
            jax.ShapeDtypeStruct(grad.shape, F32),
        ),
        in_specs=[bspec, gspec],
        out_specs=(bspec, gspec),
        name="finish",
    )(block, grad)
    return block.reshape(ex, ey, ez, ch), grad


def solution(mesh):
    nx, ny = mesh.shape["gx"], mesh.shape["gy"]
    in_specs = (
        P("gx", "gy", None, None),
        P("gx", "gy", None, None),
        P(),
        P("gy", None),
        P("gy", None),
    )
    out_specs = (P("gx", "gy", None, None), P("gy", None))
    return jax.shard_map(
        functools.partial(shards, nx, ny),
        mesh=mesh, in_specs=in_specs, out_specs=out_specs, check_vma=False,
    )
```

```python
import functools
import math

import jax
import jax.numpy as jnp
from jax import lax
from jax.experimental import pallas as pl
from jax.experimental.pallas import tpu as pltpu
from jax.sharding import PartitionSpec as P

HEADS = 12
HD = 32
WIN = 8
HALF = WIN // 2
INNER = HEADS * HD
FG = 3
FH = HEADS // FG
FC = FH * HD
GROUPS = (
    ((0, 0, 2), (1, 0, 2), (2, 0, 4)),
    ((0, 2, 2), (1, 2, 2), (2, 4, 4)),
    ((0, 4, 4), (1, 4, 4)),
    ((0, 8, 2), (1, 8, 2), (2, 8, 4)),
    ((0, 10, 2), (1, 10, 2)),
)
SPREAD = (True, True, True, True, True)
F32 = jnp.float32
BF16 = jnp.bfloat16
MESH = pl.DeviceIdType.MESH
norm_eps = 1e-05


def dot(a, b, ca, cb):
    return lax.dot_general(a, b, (((ca,), (cb,)), ((), ())), preferred_element_type=F32)


def flat_rows(x):
    rows = math.prod(x.shape[:-1])
    if x.shape[-2] % 16 == 0:
        return x.reshape(rows, x.shape[-1])
    return x.astype(F32).reshape(rows, x.shape[-1]).astype(BF16)


def width(group):
    return sum(n for _, _, n in group) * HD


def kernel(nx, ny, spread, wsplit, psplit, loss_scale, tok, tgt, gain, wq, wp, out, grad, *scratch):
    (win, thome, tph, tpw, aw, ah, wbuf, pbuf, projb, xt, qkvt, ebuf, rinv, ot, dot_t, dgrp, outv) = scratch[:17]
    ng = len(GROUPS)
    bufs = [scratch[17 + 7 * i:24 + 7 * i] for i in range(ng)]
    ssem, rsem, lsem = scratch[17 + 7 * ng:]
    nz = nx // 2
    x = lax.axis_index("gx")
    y = lax.axis_index("gy")
    core = lax.rem(x, 2)
    sib = x + 1 - 2 * core
    z = x // 2
    zodd = lax.rem(z, 2)
    zmate = x + 2 - 4 * zodd
    zpair = wsplit == 4
    whalf = wsplit // 2
    ppart = core if psplit == 2 else 0
    counter = [0]

    def gxi(d):
        return lax.rem(x + d + nx, nx)

    def gyi(d):
        return lax.rem(y + d + ny, ny)

    def remote(src, dst, dev):
        k = counter[0]
        counter[0] += 1
        return pltpu.make_async_remote_copy(
            src_ref=src, dst_ref=dst, send_sem=ssem.at[k], recv_sem=rsem.at[k],
            device_id=dev, device_id_type=MESH,
        )

    sent = []

    def go(copies):
        for c in copies:
            c.start()
            sent.append(c)

    peers = [(x, gyi(d)) for d in range(1, ny)]
    peers += [(gxi(1), y), (gxi(-1), y)]
    peers += [(gxi(2 * d), y) for d in range(1, nz)]
    side = 1 - 2 * core
    peers += [(gxi(1), gyi(side)), (gxi(-1), gyi(side))]
    barrier = pltpu.get_barrier_semaphore()
    for dev in peers:
        pl.semaphore_signal(barrier, inc=1, device_id=dev, device_id_type=MESH)
    lcount = [0]

    def local(src, dst):
        k = lcount[0]
        lcount[0] += 1
        c = pltpu.make_async_copy(src, dst, lsem.at[k])
        c.start()
        return c

    w_own = [
        [
            local(
                wq.at[:, :, pl.ds(part * INNER + g * FC, FC)],
                wbuf.at[g, y, :, :, pl.ds(part * FC, FC)],
            )
            for part in range(3)
        ]
        for g in range(FG)
    ]
    zc, pcols = pbuf.shape[2], pbuf.shape[4]
    p_own = [local(wp.at[:, :, pl.ds(k * pcols, pcols)], pbuf.at[y, :, k]) for k in range(zc)]
    own_tok = local(tok.at[pl.ds(HALF, HALF), 1 - core], win.at[0])
    own_tgt = local(tgt, thome)
    for c in w_own[0] + p_own:
        c.wait()
    pl.semaphore_wait(barrier, len(peers))

    quarters = [(0, 1), (1, 0), (1, 1)]

    def to_windows(home, wins):
        copies = []
        for a, b in quarters:
            host = 1 - core if a else core
            src = home.at[pl.ds(HALF * (1 - a), HALF), host if b else 1 - host]
            dev = (gxi(-a), gyi(2 * host - 1) if b else y)
            copies.append(remote(src, wins.at[2 * a + b], dev))
        return copies

    relay = ny == 4 and zpair and psplit == 2
    items = (0, FG, *range(1, FG))
    tail = FG - 1

    def piece(it, yy, mine):
        if it == FG:
            if zpair:
                return pbuf.at[yy, ppart, zodd if mine else 1 - zodd]
            return pbuf.at[yy, ppart, 0]
        if zpair and it != tail:
            return wbuf.at[it, yy, 2 * core + (zodd if mine else 1 - zodd)]
        return wbuf.at[it, yy, pl.ds(core * whalf, whalf)]

    def send(it, yy, mine, dev):
        part = piece(it, yy, mine)
        c = remote(part, part, dev)
        go([c])
        return c

    y1 = y + 1 - 2 * lax.rem(y, 2)
    y2 = gyi(2)
    y3 = ny - 1 - y
    tok_copies = to_windows(tok, win)
    hop = {}
    near = [gyi(d) for d in range(1, ny)]
    go(tok_copies[1:2])
    if relay:
        for it in items:
            if it not in (0, FG):
                for c in w_own[it]:
                    c.wait()
            if it == tail:
                go([tok_copies[2], tok_copies[0]])
            hop["x", it] = send(it, y, True, (x, y1))
            hop["y", it] = send(it, y, True, (x, y2))
    else:
        for it in items:
            if it not in (0, FG):
                for c in w_own[it]:
                    c.wait()
            if it == 1:
                go([tok_copies[0], tok_copies[2]])
            hop["y", it] = [send(it, y, True, (x, dev)) for dev in near]

    def norm(q):
        v = win[q].reshape(-1, win.shape[-1]).astype(F32)
        mean = jnp.mean(v, -1, keepdims=True)
        cen = v - mean
        var = jnp.mean(cen * cen, -1, keepdims=True)
        nrm = cen * lax.rsqrt(var + norm_eps) * gain[...].reshape(1, -1)
        rows = v.shape[0]
        xt[:, q * rows:(q + 1) * rows] = nrm.T.astype(BF16)

    landed = {it: [] for it in items}

    def onward(it, yy, zsend=True):
        if zsend:
            hop["z", it] = hop.get(("z", it), []) + [(yy, send(it, yy, True, (zmate, y)))]
        landed[it].append(send(it, yy, True, (sib, y)))

    def first_hops(it, zsend):
        hop["x", it].wait_recv()
        hop["d", it] = send(it, y1, True, (x, y2))
        onward(it, y1, zsend)
        hop["y", it].wait_recv()
        onward(it, y2, zsend)

    def last_hops(it):
        for yy, c in hop["z", it]:
            c.wait_recv()
            landed[it].append(send(it, yy, False, (sib, y)))

    def settle(it):
        for c in landed[it]:
            c.wait_recv()

    own_tok.wait()
    norm(0)
    if relay:
        for it in (0, FG):
            first_hops(it, True)
        for it in range(1, tail):
            first_hops(it, False)
        tok_copies[1].wait_recv()
        norm(2)
        for it in (0, FG):
            hop["d", it].wait_recv()
            onward(it, y3)
        for it in range(1, tail):
            hop["z", it] = [(yy, send(it, yy, True, (zmate, y))) for yy in (y1, y2)]
            hop["d", it].wait_recv()
            onward(it, y3)
        for it in (0, FG):
            last_hops(it)
        tok_copies[2].wait_recv()
        norm(3)
        tok_copies[0].wait_recv()
        norm(1)
    else:
        for it in (0, FG):
            for d in range(1, ny):
                hop["y", it][d - 1].wait_recv()
                if it < FG or psplit == 2:
                    landed[it].append(send(it, gyi(-d), True, (sib, y)))
        for t in (1, 0, 2):
            tok_copies[t].wait_recv()
            norm(quarters[t][0] * 2 + quarters[t][1])

    def late(it):
        if relay and it == tail:
            hop["y", it].wait_recv()
            onward(it, y2, False)
            hop["d", it].wait_recv()
            onward(it, y3, False)
        elif relay:
            last_hops(it)
        else:
            for d in range(1, ny):
                hop["y", it][d - 1].wait_recv()
                landed[it].append(send(it, gyi(-d), True, (sib, y)))

    settle(FG)
    for k in range(zc):
        projb[:, k * pcols:(k + 1) * pcols] = flat_rows(pbuf[:, :, k])
    own_tgt.wait()
    n_tok = xt.shape[1]
    tph[...] = dot(thome[...].reshape(n_tok, -1), projb[...], 1, 1).astype(BF16).reshape(tph.shape)
    t_copies = to_windows(tph, tpw)
    go(t_copies)
    own_t = local(tph.at[pl.ds(HALF, HALF), 1 - core], tpw.at[0])
    gw3 = 3 * FC

    def qkv(g):
        settle(g)
        qkvt[g * gw3:(g + 1) * gw3, :] = dot(flat_rows(wbuf[g]), xt[...], 0, 0).astype(BF16)

    if relay:
        hop["x", tail].wait_recv()
        hop["d", tail] = send(tail, y1, True, (x, y2))
        onward(tail, y1, False)
    qkv(0)

    scale = HD ** (-0.5)
    c2 = scale * math.log2(math.e)

    def rows_of(h, base=0):
        return pl.ds(pl.multiple_of(base + h * HD, HD), HD)

    def load_qkv(part, g, t):
        return qkvt[rows_of(t, g * gw3 + part * FC), :]

    def fwd(g, lo, hi):
        def body(t, carry):
            q, k, v = [load_qkv(part, g, t) for part in range(3)]
            h = g * FH + t
            s = dot(k, q, 0, 0)
            m = jnp.max(s, 0, keepdims=True)
            e = jnp.exp2((s - m) * c2)
            eb = e.astype(BF16)
            ebuf[h] = eb
            ones = jnp.ones((16, v.shape[1]), BF16)
            mixed = dot(jnp.concatenate([v, ones], 0), eb, 1, 0)
            r = 1.0 / mixed[HD:HD + 1]
            rinv[h] = r
            ot[rows_of(h), :] = mixed[:HD] * r
            return carry

        lax.fori_loop(lo, hi, body, 0, unroll=2)

    for g in range(FG):
        fwd(g, 0, FH // 2)
        if g + 1 < FG:
            late(g + 1)
        fwd(g, FH // 2, FH)
        if g + 1 < FG:
            qkv(g + 1)

    attn = ot[...].T.astype(BF16)
    aw[...] = attn.reshape(aw.shape)
    o_copies = [
        remote(
            aw.at[2 * a + b],
            ah.at[pl.ds(HALF * (1 - a), HALF), core if b else 1 - core],
            (gxi(a), gyi(side) if b else y),
        )
        for a, b in quarters
    ]
    go(o_copies)
    own_a = local(aw.at[0], ah.at[pl.ds(HALF, HALF), 1 - core])
    res = dot(attn, projb[...], 1, 0).astype(BF16)
    back = dot(res, projb[...], 1, 1)
    for c in t_copies:
        c.wait_recv()
    own_t.wait()
    tw = tpw[...].reshape(n_tok, -1).astype(F32)
    dot_t[...] = ((back - tw) * loss_scale).T.astype(BF16)

    def bwd(h0, n, dq=None, dk=None, dv=None):
        g, t0 = h0 // FH, h0 % FH

        def body(i, carry):
            q, k, v = [load_qkv(part, g, t0 + i) for part in range(3)]
            h = h0 + i
            eb = ebuf[h]
            do = dot_t[rows_of(h), :].astype(F32) * rinv[h]
            dob = do.astype(BF16)
            if dq is not None:
                rd = jnp.sum(do * ot[rows_of(h), :], 0, keepdims=True)
                dp = dot(v, dob, 0, 0)
                ds = (eb.astype(F32) * (dp - rd)).astype(BF16)
                dgrp[rows_of(i, dq), :] = (dot(k, ds, 1, 0) * scale).astype(BF16)
                dgrp[rows_of(i, dk), :] = (dot(q, ds, 1, 1) * scale).astype(BF16)
            if dv is not None:
                dgrp[rows_of(i, dv), :] = dot(dob, eb, 1, 1).astype(BF16)
            return carry

        lax.fori_loop(0, n, body, 0, unroll=n)

    st = {}

    def stage_a(i):
        snd1, rcv1 = bufs[i][:2]
        gw = width(GROUPS[i])
        dw = dot(xt[...], dgrp[:gw, :], 1, 1)
        dw = dw.reshape(ny, 2, snd1.shape[2], gw).astype(BF16)
        for cc in range(2):
            snd1[cc] = dw[:, cc]
        st["a", i] = [remote(snd1.at[1 - core], rcv1, (sib, y))]
        go(st["a", i])

    def stage_b(i):
        snd1, rcv1, s1, rcv2 = bufs[i][:4]
        for c in st["a", i]:
            c.wait_recv()
        s1[...] = (snd1[core].astype(F32) + rcv1[...].astype(F32)).astype(BF16)
        st["b", i] = [remote(s1.at[gyi(d)], rcv2.at[d - 1], (x, gyi(d))) for d in range(1, ny)]
        go(st["b", i])

    def stage_c(i):
        s1, rcv2, snd3, rcv3 = bufs[i][2:6]
        acc = s1[y].astype(F32)
        for d in range(1, ny):
            st["b", i][d - 1].wait_recv()
            acc = acc + rcv2[d - 1].astype(F32)
        snd3[...] = acc.reshape(snd3.shape).astype(BF16)
        copies = []
        for d in range(1, nz):
            piece = lax.rem(z + d, nz) if spread[i] else 0
            copies.append(remote(snd3.at[piece], rcv3.at[d - 1], (gxi(2 * d), y)))
        st["c", i] = copies
        go(copies)

    def stage_d(i):
        snd3, rcv3, fin = bufs[i][4:]
        piece = z if spread[i] else 0
        acc = snd3[piece].astype(F32)
        for d in range(1, nz):
            st["c", i][d - 1].wait_recv()
            acc = acc + rcv3[d - 1].astype(F32)
        fin[core, piece] = acc.astype(BF16)
        st["d", i] = []
        if spread[i]:
            mine = fin.at[core, z]
            st["d", i] = [remote(mine, mine, (gxi(2 * d), y)) for d in range(1, nz)]
            go(st["d", i])

    def stage_e(i):
        fin = bufs[i][6]
        for c in st["d", i]:
            c.wait_recv()
        st["e", i] = [remote(fin.at[core], fin.at[core], (sib, y))]
        go(st["e", i])

    def stage_f(i):
        for c in st["e", i]:
            c.wait_recv()
        res = flat_rows(bufs[i][6][...])
        at = 0
        for part, h0, n in GROUPS[i]:
            lo = part * INNER + h0 * HD
            grad[:, lo:lo + n * HD] = res[:, at:at + n * HD]
            at += n * HD

    def values(h0, at):
        bwd(h0, 4, None, None, at)

    bwd(0, 2, 0, 2 * HD)
    values(0, FC)
    stage_a(0)
    bwd(2, 2, 0, 2 * HD)
    stage_b(0)
    values(4, FC)
    stage_a(1)
    bwd(4, 2, 0, FC)
    stage_b(1)
    bwd(6, 2, 2 * HD, FC + 2 * HD)
    stage_a(2)
    bwd(8, 2, 0, 2 * HD)
    stage_b(2)
    values(8, FC)
    stage_a(3)
    stage_c(0)
    bwd(10, 2, 0, 2 * HD)
    stage_b(3)
    stage_a(4)
    for c in o_copies:
        c.wait_recv()
    own_a.wait()
    outv[...] = dot(ah[...].reshape(n_tok, -1), projb[...], 1, 0).astype(BF16)
    put = local(outv, out)
    stage_c(1)
    stage_b(4)
    stage_d(0)
    stage_c(2)
    stage_d(1)
    stage_c(3)
    stage_c(4)
    stage_e(0)
    stage_d(2)
    stage_e(1)
    stage_f(0)
    stage_d(3)
    stage_f(1)
    stage_d(4)
    stage_e(4)
    stage_e(2)
    stage_e(3)
    stage_f(4)
    stage_f(2)
    stage_f(3)
    put.wait()
    for c in sent:
        c.wait_send()


def finish(b_in, g_in, b_out, g_out):
    b_out[...] = b_in[...]
    g_out[...] = g_in[...].astype(F32)


def shards(nx, ny, tokens, target, norm_gain, qkv_weight, proj_weight):
    ex, ey, ez, ch = tokens.shape
    rows = HALF * ez
    wr = qkv_weight.shape[0]
    pr = proj_weight.shape[0]
    wsplit = 4 if wr % 64 == 0 else 2
    psplit = 2 if pr % 32 == 0 else 1
    zc = 2 if wsplit == 4 else 1
    hr = wr // 2
    nz = nx // 2
    spread = [hr % (8 * nz) == 0 and on for on in SPREAD]
    n_tok = ex * ey * ez
    inner3 = qkv_weight.shape[1]
    loss_scale = 2.0 / math.sqrt(n_tok * nx * ny)
    ncopies = 9 + (FG + 1) * max(12, 2 * (ny - 1))
    ncopies += sum(2 + (ny - 1) + (nz - 1) * (2 if on else 1) for on in spread)
    any_spec = pl.BlockSpec(memory_space=pl.ANY)
    vm_spec = pl.BlockSpec(memory_space=pltpu.VMEM)
    group_bufs = []
    for group, on in zip(GROUPS, spread):
        gw = width(group)
        pieces = nz if on else 1
        prow = hr // pieces
        group_bufs += [
            pltpu.VMEM((2, ny, hr, gw), BF16),
            pltpu.VMEM((ny, hr, gw), BF16),
            pltpu.VMEM((ny, hr, gw), BF16),
            pltpu.VMEM((ny - 1, hr, gw), BF16),
            pltpu.VMEM((pieces, prow, gw), BF16),
            pltpu.VMEM((nz - 1, prow, gw), BF16),
            pltpu.VMEM((2, pieces, prow, gw), BF16),
        ]
    block, grad = pl.pallas_call(
        functools.partial(kernel, nx, ny, spread, wsplit, psplit, loss_scale),
        out_shape=(
            jax.ShapeDtypeStruct((n_tok, ch), BF16),
            jax.ShapeDtypeStruct((wr, inner3), BF16),
        ),
        in_specs=[any_spec, any_spec, vm_spec, any_spec, any_spec],
        out_specs=(any_spec, vm_spec),
        scratch_shapes=[
            pltpu.VMEM((4, HALF, rows, ch), BF16),
            pltpu.VMEM((ex, 2, rows, ch), BF16),
            pltpu.VMEM((ex, 2, rows, INNER), BF16),
            pltpu.VMEM((4, HALF, rows, INNER), BF16),
            pltpu.VMEM((4, HALF, rows, INNER), BF16),
            pltpu.VMEM((ex, 2, rows, INNER), BF16),
            pltpu.VMEM((FG, ny, wsplit, wr // wsplit, 3 * FC), BF16),
            pltpu.VMEM((ny, psplit, zc, pr // psplit, ch // zc), BF16),
            pltpu.VMEM((INNER, ch), BF16),
            pltpu.VMEM((ch, n_tok), BF16),
            pltpu.VMEM((inner3, n_tok), BF16),
            pltpu.VMEM((HEADS, n_tok, n_tok), BF16),
            pltpu.VMEM((HEADS, 1, n_tok), F32),
            pltpu.VMEM((INNER, n_tok), F32),
            pltpu.VMEM((INNER, n_tok), BF16),
            pltpu.VMEM((3 * FC, n_tok), BF16),
            pltpu.VMEM((n_tok, ch), BF16),
            *group_bufs,
            pltpu.SemaphoreType.DMA((ncopies,)),
            pltpu.SemaphoreType.DMA((ncopies,)),
            pltpu.SemaphoreType.DMA((3 * FG + 7,)),
        ],
        compiler_params=pltpu.CompilerParams(
            collective_id=0, has_side_effects=True, vmem_limit_bytes=60 * 2**20
        ),
        name="step",
    )(
        tokens.reshape(ex, 2, rows, ch),
        target.reshape(ex, 2, rows, ch),
        norm_gain,
        qkv_weight.reshape(wsplit, wr // wsplit, inner3),
        proj_weight.reshape(psplit, pr // psplit, ch),
    )
    steps = 2 if wr % 64 == 0 else 1
    bspec = pl.BlockSpec((n_tok // steps, ch), lambda i: (i, 0))
    gspec = pl.BlockSpec((wr // steps, inner3), lambda i: (i, 0))
    block, grad = pl.pallas_call(
        finish,
        grid=(steps,),
        out_shape=(
            jax.ShapeDtypeStruct(block.shape, BF16),
            jax.ShapeDtypeStruct(grad.shape, F32),
        ),
        in_specs=[bspec, gspec],
        out_specs=(bspec, gspec),
        name="finish",
    )(block, grad)
    return block.reshape(ex, ey, ez, ch), grad


def solution(mesh):
    nx, ny = mesh.shape["gx"], mesh.shape["gy"]
    in_specs = (
        P("gx", "gy", None, None),
        P("gx", "gy", None, None),
        P(),
        P("gy", None),
        P("gy", None),
    )
    out_specs = (P("gx", "gy", None, None), P("gy", None))
    return jax.shard_map(
        functools.partial(shards, nx, ny),
        mesh=mesh, in_specs=in_specs, out_specs=out_specs, check_vma=False,
    )
```

```python
import functools
import math

import jax
import jax.numpy as jnp
from jax import lax
from jax.experimental import pallas as pl
from jax.experimental.pallas import tpu as pltpu
from jax.sharding import PartitionSpec as P

HEADS = 12
HD = 32
WIN = 8
HALF = WIN // 2
INNER = HEADS * HD
FG = 3
FH = HEADS // FG
FC = FH * HD
GROUPS = (
    ((0, 0, 4), (1, 0, 4), (2, 0, 4)),
    ((0, 4, 4), (1, 4, 4), (2, 4, 4)),
    ((0, 8, 4), (1, 8, 4), (2, 8, 4)),
)
SPREAD = (True, True, True)
F32 = jnp.float32
BF16 = jnp.bfloat16
MESH = pl.DeviceIdType.MESH
norm_eps = 1e-05


def dot(a, b, ca, cb):
    return lax.dot_general(a, b, (((ca,), (cb,)), ((), ())), preferred_element_type=F32)


def flat_rows(x):
    rows = math.prod(x.shape[:-1])
    if x.shape[-2] % 16 == 0:
        return x.reshape(rows, x.shape[-1])
    return x.astype(F32).reshape(rows, x.shape[-1]).astype(BF16)


def width(group):
    return sum(n for _, _, n in group) * HD


def kernel(nx, ny, spread, wsplit, psplit, loss_scale, tok, tgt, gain_in, wq, wp, out, grad, *scratch):
    (win, thome, tph, tpw, aw, ah, wbuf, pbuf, projb, xt, qkvt, ebuf, rinv, ot, dot_t, dgrp, outv, gain) = scratch[:18]
    ng = len(GROUPS)
    bufs = [scratch[18 + 7 * i:25 + 7 * i] for i in range(ng)]
    ssem, rsem, lsem = scratch[18 + 7 * ng:]
    nz = nx // 2
    x = lax.axis_index("gx")
    y = lax.axis_index("gy")
    core = lax.rem(x, 2)
    sib = x + 1 - 2 * core
    z = x // 2
    zodd = lax.rem(z, 2)
    zmate = x + 2 - 4 * zodd
    zpair = wsplit == 4
    whalf = wsplit // 2
    ppart = core if psplit == 2 else 0
    counter = [0]

    def gxi(d):
        return lax.rem(x + d + nx, nx)

    def gyi(d):
        return lax.rem(y + d + ny, ny)

    def remote(src, dst, dev):
        k = counter[0]
        counter[0] += 1
        return pltpu.make_async_remote_copy(
            src_ref=src, dst_ref=dst, send_sem=ssem.at[k], recv_sem=rsem.at[k],
            device_id=dev, device_id_type=MESH,
        )

    sent = []

    def go(copies):
        for c in copies:
            c.start()
            sent.append(c)

    peers = [(x, gyi(d)) for d in range(1, ny)]
    peers += [(gxi(1), y), (gxi(-1), y)]
    peers += [(gxi(2 * d), y) for d in range(1, nz)]
    side = 1 - 2 * core
    peers += [(gxi(1), gyi(side)), (gxi(-1), gyi(side))]
    barrier = pltpu.get_barrier_semaphore()
    for dev in peers:
        pl.semaphore_signal(barrier, inc=1, device_id=dev, device_id_type=MESH)
    lcount = [0]

    def local(src, dst):
        k = lcount[0]
        lcount[0] += 1
        c = pltpu.make_async_copy(src, dst, lsem.at[k])
        c.start()
        return c

    w_own = [
        [
            local(
                wq.at[:, :, pl.ds(part * INNER + g * FC, FC)],
                wbuf.at[g, y, :, :, pl.ds(part * FC, FC)],
            )
            for part in range(3)
        ]
        for g in range(FG)
    ]
    zc, pcols = pbuf.shape[2], pbuf.shape[4]
    p_own = [local(wp.at[:, :, pl.ds(k * pcols, pcols)], pbuf.at[y, :, k]) for k in range(zc)]
    own_gain = local(gain_in, gain)
    own_tok = local(tok.at[pl.ds(HALF, HALF), 1 - core], win.at[0])
    own_tgt = local(tgt, thome)
    for c in w_own[0] + p_own:
        c.wait()
    pl.semaphore_wait(barrier, len(peers))

    quarters = [(0, 1), (1, 0), (1, 1)]

    def to_windows(home, wins):
        copies = []
        for a, b in quarters:
            host = 1 - core if a else core
            src = home.at[pl.ds(HALF * (1 - a), HALF), host if b else 1 - host]
            dev = (gxi(-a), gyi(2 * host - 1) if b else y)
            copies.append(remote(src, wins.at[2 * a + b], dev))
        return copies

    relay = ny == 4 and zpair and psplit == 2
    items = (0, FG, *range(1, FG))
    tail = FG - 1

    def piece(it, yy, mine):
        if it == FG:
            if zpair:
                return pbuf.at[yy, ppart, zodd if mine else 1 - zodd]
            return pbuf.at[yy, ppart, 0]
        if zpair and it != tail:
            return wbuf.at[it, yy, 2 * core + (zodd if mine else 1 - zodd)]
        return wbuf.at[it, yy, pl.ds(core * whalf, whalf)]

    def send(it, yy, mine, dev):
        part = piece(it, yy, mine)
        c = remote(part, part, dev)
        go([c])
        return c

    y1 = y + 1 - 2 * lax.rem(y, 2)
    y2 = gyi(2)
    y3 = ny - 1 - y
    tok_copies = to_windows(tok, win)
    hop = {}
    near = [gyi(d) for d in range(1, ny)]
    go(tok_copies[1:2])
    if relay:
        for it in items:
            if it not in (0, FG):
                for c in w_own[it]:
                    c.wait()
            if it == tail:
                go([tok_copies[2], tok_copies[0]])
            hop["x", it] = send(it, y, True, (x, y1))
            hop["y", it] = send(it, y, True, (x, y2))
    else:
        for it in items:
            if it not in (0, FG):
                for c in w_own[it]:
                    c.wait()
            if it == 1:
                go([tok_copies[0], tok_copies[2]])
            hop["y", it] = [send(it, y, True, (x, dev)) for dev in near]

    def norm(q):
        v = win[q].reshape(-1, win.shape[-1]).astype(F32)
        mean = jnp.mean(v, -1, keepdims=True)
        cen = v - mean
        var = jnp.mean(cen * cen, -1, keepdims=True)
        nrm = cen * lax.rsqrt(var + norm_eps) * gain[...].reshape(1, -1)
        rows = v.shape[0]
        xt[:, q * rows:(q + 1) * rows] = nrm.T.astype(BF16)

    landed = {it: [] for it in items}

    def onward(it, yy, zsend=True):
        if zsend:
            hop["z", it] = hop.get(("z", it), []) + [(yy, send(it, yy, True, (zmate, y)))]
        landed[it].append(send(it, yy, True, (sib, y)))

    def first_hops(it, zsend):
        hop["x", it].wait_recv()
        hop["d", it] = send(it, y1, True, (x, y2))
        onward(it, y1, zsend)
        hop["y", it].wait_recv()
        onward(it, y2, zsend)

    def last_hops(it):
        for yy, c in hop["z", it]:
            c.wait_recv()
            landed[it].append(send(it, yy, False, (sib, y)))

    def settle(it):
        for c in landed[it]:
            c.wait_recv()

    own_gain.wait()
    own_tok.wait()
    norm(0)
    if relay:
        for it in (0, FG):
            first_hops(it, True)
        for it in range(1, tail):
            first_hops(it, False)
        tok_copies[1].wait_recv()
        norm(2)
        for it in (0, FG):
            hop["d", it].wait_recv()
            onward(it, y3)
        for it in range(1, tail):
            hop["z", it] = [(yy, send(it, yy, True, (zmate, y))) for yy in (y1, y2)]
            hop["d", it].wait_recv()
            onward(it, y3)
        for it in (0, FG):
            last_hops(it)
        tok_copies[2].wait_recv()
        norm(3)
        tok_copies[0].wait_recv()
        norm(1)
    else:
        for it in (0, FG):
            for d in range(1, ny):
                hop["y", it][d - 1].wait_recv()
                if it < FG or psplit == 2:
                    landed[it].append(send(it, gyi(-d), True, (sib, y)))
        for t in (1, 0, 2):
            tok_copies[t].wait_recv()
            norm(quarters[t][0] * 2 + quarters[t][1])

    def late(it):
        if relay and it == tail:
            hop["y", it].wait_recv()
            onward(it, y2, False)
            hop["d", it].wait_recv()
            onward(it, y3, False)
        elif relay:
            last_hops(it)
        else:
            for d in range(1, ny):
                hop["y", it][d - 1].wait_recv()
                landed[it].append(send(it, gyi(-d), True, (sib, y)))

    settle(FG)
    for k in range(zc):
        projb[:, k * pcols:(k + 1) * pcols] = flat_rows(pbuf[:, :, k])
    own_tgt.wait()
    n_tok = xt.shape[1]
    tph[...] = dot(thome[...].reshape(n_tok, -1), projb[...], 1, 1).astype(BF16).reshape(tph.shape)
    t_copies = to_windows(tph, tpw)
    go(t_copies)
    own_t = local(tph.at[pl.ds(HALF, HALF), 1 - core], tpw.at[0])
    gw3 = 3 * FC

    def qkv(g):
        settle(g)
        qkvt[g * gw3:(g + 1) * gw3, :] = dot(flat_rows(wbuf[g]), xt[...], 0, 0).astype(BF16)

    if relay:
        hop["x", tail].wait_recv()
        hop["d", tail] = send(tail, y1, True, (x, y2))
        onward(tail, y1, False)
    qkv(0)

    scale = HD ** (-0.5)
    c2 = scale * math.log2(math.e)

    def rows_of(h, base=0):
        return pl.ds(pl.multiple_of(base + h * HD, HD), HD)

    def load_qkv(part, g, t):
        return qkvt[rows_of(t, g * gw3 + part * FC), :]

    def fwd(g, lo, hi):
        def body(t, carry):
            q, k, v = [load_qkv(part, g, t) for part in range(3)]
            h = g * FH + t
            s = dot(k, q, 0, 0)
            m = jnp.max(s, 0, keepdims=True)
            e = jnp.exp2((s - m) * c2)
            eb = e.astype(BF16)
            ebuf[h] = eb
            ones = jnp.ones((16, v.shape[1]), BF16)
            mixed = dot(jnp.concatenate([v, ones], 0), eb, 1, 0)
            r = 1.0 / mixed[HD:HD + 1]
            rinv[h] = r
            ot[rows_of(h), :] = mixed[:HD] * r
            return carry

        lax.fori_loop(lo, hi, body, 0, unroll=2)

    for g in range(FG):
        fwd(g, 0, FH // 2)
        if g + 1 < FG:
            late(g + 1)
        fwd(g, FH // 2, FH)
        if g + 1 < FG:
            qkv(g + 1)

    attn = ot[...].T.astype(BF16)
    aw[...] = attn.reshape(aw.shape)
    o_copies = [
        remote(
            aw.at[2 * a + b],
            ah.at[pl.ds(HALF * (1 - a), HALF), core if b else 1 - core],
            (gxi(a), gyi(side) if b else y),
        )
        for a, b in quarters
    ]
    go(o_copies)
    own_a = local(aw.at[0], ah.at[pl.ds(HALF, HALF), 1 - core])
    res = dot(attn, projb[...], 1, 0).astype(BF16)
    back = dot(res, projb[...], 1, 1)
    for c in t_copies:
        c.wait_recv()
    own_t.wait()
    tw = tpw[...].reshape(n_tok, -1).astype(F32)
    dot_t[...] = ((back - tw) * loss_scale).T.astype(BF16)

    def bwd(h0, n, dq=None, dk=None, dv=None):
        g, t0 = h0 // FH, h0 % FH

        def body(i, carry):
            q, k, v = [load_qkv(part, g, t0 + i) for part in range(3)]
            h = h0 + i
            eb = ebuf[h]
            do = dot_t[rows_of(h), :].astype(F32) * rinv[h]
            dob = do.astype(BF16)
            if dq is not None:
                rd = jnp.sum(do * ot[rows_of(h), :], 0, keepdims=True)
                dp = dot(v, dob, 0, 0)
                ds = (eb.astype(F32) * (dp - rd)).astype(BF16)
                dgrp[rows_of(i, dq), :] = (dot(k, ds, 1, 0) * scale).astype(BF16)
                dgrp[rows_of(i, dk), :] = (dot(q, ds, 1, 1) * scale).astype(BF16)
            if dv is not None:
                dgrp[rows_of(i, dv), :] = dot(dob, eb, 1, 1).astype(BF16)
            return carry

        lax.fori_loop(0, n, body, 0, unroll=n)

    st = {}

    def stage_a(i):
        snd1, rcv1 = bufs[i][:2]
        gw = width(GROUPS[i])
        dw = dot(xt[...], dgrp[:gw, :], 1, 1)
        dw = dw.reshape(ny, 2, snd1.shape[2], gw).astype(BF16)
        for cc in range(2):
            snd1[cc] = dw[:, cc]
        st["a", i] = [remote(snd1.at[1 - core], rcv1, (sib, y))]
        go(st["a", i])

    def stage_b(i):
        snd1, rcv1, s1, rcv2 = bufs[i][:4]
        for c in st["a", i]:
            c.wait_recv()
        s1[...] = (snd1[core].astype(F32) + rcv1[...].astype(F32)).astype(BF16)
        st["b", i] = [remote(s1.at[gyi(d)], rcv2.at[d - 1], (x, gyi(d))) for d in range(1, ny)]
        go(st["b", i])

    def stage_c(i):
        s1, rcv2, snd3, rcv3 = bufs[i][2:6]
        acc = s1[y].astype(F32)
        for d in range(1, ny):
            st["b", i][d - 1].wait_recv()
            acc = acc + rcv2[d - 1].astype(F32)
        snd3[...] = acc.reshape(snd3.shape).astype(BF16)
        copies = []
        for d in range(1, nz):
            piece = lax.rem(z + d, nz) if spread[i] else 0
            copies.append(remote(snd3.at[piece], rcv3.at[d - 1], (gxi(2 * d), y)))
        st["c", i] = copies
        go(copies)

    def stage_d(i):
        snd3, rcv3, fin = bufs[i][4:]
        piece = z if spread[i] else 0
        acc = snd3[piece].astype(F32)
        for d in range(1, nz):
            st["c", i][d - 1].wait_recv()
            acc = acc + rcv3[d - 1].astype(F32)
        fin[core, piece] = acc.astype(BF16)
        st["d", i] = []
        if spread[i]:
            mine = fin.at[core, z]
            st["d", i] = [remote(mine, mine, (gxi(2 * d), y)) for d in range(1, nz)]
            go(st["d", i])

    def stage_e(i):
        fin = bufs[i][6]
        for c in st["d", i]:
            c.wait_recv()
        st["e", i] = [remote(fin.at[core], fin.at[core], (sib, y))]
        go(st["e", i])

    def stage_f(i):
        for c in st["e", i]:
            c.wait_recv()
        res = flat_rows(bufs[i][6][...])
        at = 0
        for part, h0, n in GROUPS[i]:
            lo = part * INNER + h0 * HD
            grad[:, lo:lo + n * HD] = res[:, at:at + n * HD]
            at += n * HD

    def values(h0, at):
        bwd(h0, 4, None, None, at)

    bwd(0, 4, 0, FC, 2 * FC)
    stage_a(0)
    bwd(4, 2, 0, FC, 2 * FC)
    stage_b(0)
    bwd(6, 2, 2 * HD, FC + 2 * HD, 2 * FC + 2 * HD)
    stage_a(1)
    bwd(8, 2, 0, FC, 2 * FC)
    stage_b(1)
    bwd(10, 2, 2 * HD, FC + 2 * HD, 2 * FC + 2 * HD)
    stage_a(2)
    stage_c(0)
    stage_b(2)
    for c in o_copies:
        c.wait_recv()
    own_a.wait()
    outv[...] = dot(ah[...].reshape(n_tok, -1), projb[...], 1, 0).astype(BF16)
    put = local(outv, out)
    stage_c(1)
    stage_d(0)
    stage_d(1)
    stage_c(2)
    stage_e(0)
    stage_e(1)
    stage_d(2)
    stage_f(0)
    stage_f(1)
    stage_e(2)
    stage_f(2)
    put.wait()
    for c in sent:
        c.wait_send()


def finish(b_in, g_in, b_out, g_out):
    b_out[...] = b_in[...]
    g_out[...] = g_in[...].astype(F32)


def shards(nx, ny, tokens, target, norm_gain, qkv_weight, proj_weight):
    ex, ey, ez, ch = tokens.shape
    rows = HALF * ez
    wr = qkv_weight.shape[0]
    pr = proj_weight.shape[0]
    wsplit = 4 if wr % 64 == 0 else 2
    psplit = 2 if pr % 32 == 0 else 1
    zc = 2 if wsplit == 4 else 1
    hr = wr // 2
    nz = nx // 2
    spread = [hr % (8 * nz) == 0 and on for on in SPREAD]
    n_tok = ex * ey * ez
    inner3 = qkv_weight.shape[1]
    loss_scale = 2.0 / math.sqrt(n_tok * nx * ny)
    ncopies = 9 + (FG + 1) * max(12, 2 * (ny - 1))
    ncopies += sum(2 + (ny - 1) + (nz - 1) * (2 if on else 1) for on in spread)
    any_spec = pl.BlockSpec(memory_space=pl.ANY)
    vm_spec = pl.BlockSpec(memory_space=pltpu.VMEM)
    group_bufs = []
    for group, on in zip(GROUPS, spread):
        gw = width(group)
        pieces = nz if on else 1
        prow = hr // pieces
        group_bufs += [
            pltpu.VMEM((2, ny, hr, gw), BF16),
            pltpu.VMEM((ny, hr, gw), BF16),
            pltpu.VMEM((ny, hr, gw), BF16),
            pltpu.VMEM((ny - 1, hr, gw), BF16),
            pltpu.VMEM((pieces, prow, gw), BF16),
            pltpu.VMEM((nz - 1, prow, gw), BF16),
            pltpu.VMEM((2, pieces, prow, gw), BF16),
        ]
    block, grad = pl.pallas_call(
        functools.partial(kernel, nx, ny, spread, wsplit, psplit, loss_scale),
        out_shape=(
            jax.ShapeDtypeStruct((n_tok, ch), BF16),
            jax.ShapeDtypeStruct((wr, inner3), BF16),
        ),
        in_specs=[any_spec] * 5,
        out_specs=(any_spec, vm_spec),
        scratch_shapes=[
            pltpu.VMEM((4, HALF, rows, ch), BF16),
            pltpu.VMEM((ex, 2, rows, ch), BF16),
            pltpu.VMEM((ex, 2, rows, INNER), BF16),
            pltpu.VMEM((4, HALF, rows, INNER), BF16),
            pltpu.VMEM((4, HALF, rows, INNER), BF16),
            pltpu.VMEM((ex, 2, rows, INNER), BF16),
            pltpu.VMEM((FG, ny, wsplit, wr // wsplit, 3 * FC), BF16),
            pltpu.VMEM((ny, psplit, zc, pr // psplit, ch // zc), BF16),
            pltpu.VMEM((INNER, ch), BF16),
            pltpu.VMEM((ch, n_tok), BF16),
            pltpu.VMEM((inner3, n_tok), BF16),
            pltpu.VMEM((HEADS, n_tok, n_tok), BF16),
            pltpu.VMEM((HEADS, 1, n_tok), F32),
            pltpu.VMEM((INNER, n_tok), F32),
            pltpu.VMEM((INNER, n_tok), BF16),
            pltpu.VMEM((3 * FC, n_tok), BF16),
            pltpu.VMEM((n_tok, ch), BF16),
            pltpu.VMEM((ch,), F32),
            *group_bufs,
            pltpu.SemaphoreType.DMA((ncopies,)),
            pltpu.SemaphoreType.DMA((ncopies,)),
            pltpu.SemaphoreType.DMA((3 * FG + 8,)),
        ],
        compiler_params=pltpu.CompilerParams(
            collective_id=0, has_side_effects=True, vmem_limit_bytes=60 * 2**20
        ),
        name="step",
    )(
        tokens.reshape(ex, 2, rows, ch),
        target.reshape(ex, 2, rows, ch),
        norm_gain,
        qkv_weight.reshape(wsplit, wr // wsplit, inner3),
        proj_weight.reshape(psplit, pr // psplit, ch),
    )
    steps = 2 if wr % 64 == 0 else 1
    bspec = pl.BlockSpec((n_tok // steps, ch), lambda i: (i, 0))
    gspec = pl.BlockSpec((wr // steps, inner3), lambda i: (i, 0))
    block, grad = pl.pallas_call(
        finish,
        grid=(steps,),
        out_shape=(
            jax.ShapeDtypeStruct(block.shape, BF16),
            jax.ShapeDtypeStruct(grad.shape, F32),
        ),
        in_specs=[bspec, gspec],
        out_specs=(bspec, gspec),
        name="finish",
    )(block, grad)
    return block.reshape(ex, ey, ez, ch), grad


def solution(mesh):
    nx, ny = mesh.shape["gx"], mesh.shape["gy"]
    in_specs = (
        P("gx", "gy", None, None),
        P("gx", "gy", None, None),
        P(),
        P("gy", None),
        P("gy", None),
    )
    out_specs = (P("gx", "gy", None, None), P("gy", None))
    return jax.shard_map(
        functools.partial(shards, nx, ny),
        mesh=mesh, in_specs=in_specs, out_specs=out_specs, check_vma=False,
    )
```

```python
import functools
import math

import jax
import jax.numpy as jnp
from jax import lax
from jax.experimental import pallas as pl
from jax.experimental.pallas import tpu as pltpu
from jax.sharding import PartitionSpec as P

HEADS = 12
HD = 32
WIN = 8
HALF = WIN // 2
INNER = HEADS * HD
FG = 3
FH = HEADS // FG
FC = FH * HD
GROUPS = (
    ((0, 0, 4), (1, 0, 4), (2, 0, 4)),
    ((0, 4, 4), (1, 4, 4), (2, 4, 4)),
    ((0, 8, 4), (1, 8, 4), (2, 8, 4)),
)
SPREAD = (True, True, True)
F32 = jnp.float32
BF16 = jnp.bfloat16
MESH = pl.DeviceIdType.MESH
norm_eps = 1e-05


def dot(a, b, ca, cb):
    return lax.dot_general(a, b, (((ca,), (cb,)), ((), ())), preferred_element_type=F32)


def flat_rows(x):
    rows = math.prod(x.shape[:-1])
    if x.shape[-2] % 16 == 0:
        return x.reshape(rows, x.shape[-1])
    return x.astype(F32).reshape(rows, x.shape[-1]).astype(BF16)


def width(group):
    return sum(n for _, _, n in group) * HD


def kernel(nx, ny, spread, wsplit, psplit, loss_scale, tok, tgt, gain_in, wq, wp, out, grad, *scratch):
    (win, thome, tph, tpw, aw, ah, wbuf, pbuf, projb, xt, qkvt, ebuf, rinv, ot, dot_t, dgrp, outv, gain) = scratch[:18]
    ng = len(GROUPS)
    bufs = [scratch[18 + 7 * i:25 + 7 * i] for i in range(ng)]
    ssem, rsem, lsem = scratch[18 + 7 * ng:]
    nz = nx // 2
    x = lax.axis_index("gx")
    y = lax.axis_index("gy")
    core = lax.rem(x, 2)
    sib = x + 1 - 2 * core
    z = x // 2
    zodd = lax.rem(z, 2)
    zmate = x + 2 - 4 * zodd
    zpair = wsplit == 4
    whalf = wsplit // 2
    ppart = core if psplit == 2 else 0
    counter = [0]

    def gxi(d):
        return lax.rem(x + d + nx, nx)

    def gyi(d):
        return lax.rem(y + d + ny, ny)

    def remote(src, dst, dev):
        k = counter[0]
        counter[0] += 1
        return pltpu.make_async_remote_copy(
            src_ref=src, dst_ref=dst, send_sem=ssem.at[k], recv_sem=rsem.at[k],
            device_id=dev, device_id_type=MESH,
        )

    sent = []

    def go(copies):
        for c in copies:
            c.start()
            sent.append(c)

    peers = [(x, gyi(d)) for d in range(1, ny)]
    peers += [(gxi(1), y), (gxi(-1), y)]
    peers += [(gxi(2 * d), y) for d in range(1, nz)]
    side = 1 - 2 * core
    peers += [(gxi(1), gyi(side)), (gxi(-1), gyi(side))]
    barrier = pltpu.get_barrier_semaphore()
    for dev in peers:
        pl.semaphore_signal(barrier, inc=1, device_id=dev, device_id_type=MESH)
    lcount = [0]

    def local(src, dst):
        k = lcount[0]
        lcount[0] += 1
        c = pltpu.make_async_copy(src, dst, lsem.at[k])
        c.start()
        return c

    w_own = [
        [
            local(
                wq.at[:, :, pl.ds(part * INNER + g * FC, FC)],
                wbuf.at[g, y, :, :, pl.ds(part * FC, FC)],
            )
            for part in range(3)
        ]
        for g in range(FG)
    ]
    zc, pcols = pbuf.shape[2], pbuf.shape[4]
    p_own = [local(wp.at[:, :, pl.ds(k * pcols, pcols)], pbuf.at[y, :, k]) for k in range(zc)]
    own_gain = local(gain_in, gain)
    own_tok = local(tok.at[pl.ds(HALF, HALF), 1 - core], win.at[0])
    own_tgt = local(tgt, thome)
    for c in w_own[0] + p_own:
        c.wait()
    pl.semaphore_wait(barrier, len(peers))

    quarters = [(0, 1), (1, 0), (1, 1)]

    def to_windows(home, wins):
        copies = []
        for a, b in quarters:
            host = 1 - core if a else core
            src = home.at[pl.ds(HALF * (1 - a), HALF), host if b else 1 - host]
            dev = (gxi(-a), gyi(2 * host - 1) if b else y)
            copies.append(remote(src, wins.at[2 * a + b], dev))
        return copies

    relay = ny == 4 and zpair and psplit == 2
    items = (0, FG, *range(1, FG))
    tail = FG - 1

    def piece(it, yy, mine):
        if it == FG:
            if zpair:
                return pbuf.at[yy, ppart, zodd if mine else 1 - zodd]
            return pbuf.at[yy, ppart, 0]
        if zpair and it != tail:
            return wbuf.at[it, yy, 2 * core + (zodd if mine else 1 - zodd)]
        return wbuf.at[it, yy, pl.ds(core * whalf, whalf)]

    def send(it, yy, mine, dev):
        part = piece(it, yy, mine)
        c = remote(part, part, dev)
        go([c])
        return c

    y1 = y + 1 - 2 * lax.rem(y, 2)
    y2 = gyi(2)
    y3 = ny - 1 - y
    tok_copies = to_windows(tok, win)
    hop = {}
    near = [gyi(d) for d in range(1, ny)]
    go(tok_copies[1:2])
    if relay:
        for it in items:
            if it not in (0, FG):
                for c in w_own[it]:
                    c.wait()
            if it == tail:
                go([tok_copies[2], tok_copies[0]])
            hop["x", it] = send(it, y, True, (x, y1))
            hop["y", it] = send(it, y, True, (x, y2))
    else:
        for it in items:
            if it not in (0, FG):
                for c in w_own[it]:
                    c.wait()
            if it == 1:
                go([tok_copies[0], tok_copies[2]])
            hop["y", it] = [send(it, y, True, (x, dev)) for dev in near]

    def norm(q):
        v = win[q].reshape(-1, win.shape[-1]).astype(F32)
        mean = jnp.mean(v, -1, keepdims=True)
        cen = v - mean
        var = jnp.mean(cen * cen, -1, keepdims=True)
        nrm = cen * lax.rsqrt(var + norm_eps) * gain[...].reshape(1, -1)
        rows = v.shape[0]
        xt[:, q * rows:(q + 1) * rows] = nrm.T.astype(BF16)

    landed = {it: [] for it in items}

    def onward(it, yy, zsend=True):
        if zsend:
            hop["z", it] = hop.get(("z", it), []) + [(yy, send(it, yy, True, (zmate, y)))]
        landed[it].append(send(it, yy, True, (sib, y)))

    def first_hops(it, zsend):
        hop["x", it].wait_recv()
        hop["d", it] = send(it, y1, True, (x, y2))
        onward(it, y1, zsend)
        hop["y", it].wait_recv()
        onward(it, y2, zsend)

    def last_hops(it):
        for yy, c in hop["z", it]:
            c.wait_recv()
            landed[it].append(send(it, yy, False, (sib, y)))

    def settle(it):
        for c in landed[it]:
            c.wait_recv()

    own_gain.wait()
    own_tok.wait()
    norm(0)
    if relay:
        for it in (0, FG):
            first_hops(it, True)
        for it in range(1, tail):
            first_hops(it, False)
        tok_copies[1].wait_recv()
        norm(2)
        for it in (0, FG):
            hop["d", it].wait_recv()
            onward(it, y3)
        for it in range(1, tail):
            hop["z", it] = [(yy, send(it, yy, True, (zmate, y))) for yy in (y1, y2)]
            hop["d", it].wait_recv()
            onward(it, y3)
        for it in (0, FG):
            last_hops(it)
        tok_copies[2].wait_recv()
        norm(3)
        tok_copies[0].wait_recv()
        norm(1)
    else:
        for it in (0, FG):
            for d in range(1, ny):
                hop["y", it][d - 1].wait_recv()
                if it < FG or psplit == 2:
                    landed[it].append(send(it, gyi(-d), True, (sib, y)))
        for t in (1, 0, 2):
            tok_copies[t].wait_recv()
            norm(quarters[t][0] * 2 + quarters[t][1])

    def late(it):
        if relay and it == tail:
            hop["y", it].wait_recv()
            onward(it, y2, False)
            hop["d", it].wait_recv()
            onward(it, y3, False)
        elif relay:
            last_hops(it)
        else:
            for d in range(1, ny):
                hop["y", it][d - 1].wait_recv()
                landed[it].append(send(it, gyi(-d), True, (sib, y)))

    settle(FG)
    for k in range(zc):
        projb[:, k * pcols:(k + 1) * pcols] = flat_rows(pbuf[:, :, k])
    own_tgt.wait()
    n_tok = xt.shape[1]
    tph[...] = dot(thome[...].reshape(n_tok, -1), projb[...], 1, 1).astype(BF16).reshape(tph.shape)
    t_copies = to_windows(tph, tpw)
    go(t_copies)
    own_t = local(tph.at[pl.ds(HALF, HALF), 1 - core], tpw.at[0])
    gw3 = 3 * FC

    def qkv(g):
        settle(g)
        qkvt[g * gw3:(g + 1) * gw3, :] = dot(flat_rows(wbuf[g]), xt[...], 0, 0).astype(BF16)

    if relay:
        hop["x", tail].wait_recv()
        hop["d", tail] = send(tail, y1, True, (x, y2))
        onward(tail, y1, False)
    qkv(0)

    scale = HD ** (-0.5)
    c2 = scale * math.log2(math.e)

    def rows_of(h, base=0):
        return pl.ds(pl.multiple_of(base + h * HD, HD), HD)

    def load_qkv(part, g, t):
        return qkvt[rows_of(t, g * gw3 + part * FC), :]

    def fwd(g, lo, hi):
        def body(t, carry):
            q, k, v = [load_qkv(part, g, t) for part in range(3)]
            h = g * FH + t
            s = dot(k, q, 0, 0)
            m = jnp.max(s, 0, keepdims=True)
            e = jnp.exp2(s * c2 - m * c2)
            eb = e.astype(BF16)
            ebuf[h] = eb
            ones = jnp.ones((16, v.shape[1]), BF16)
            mixed = dot(jnp.concatenate([v, ones], 0), eb, 1, 0)
            r = 1.0 / mixed[HD:HD + 1]
            rinv[h] = r
            ot[rows_of(h), :] = mixed[:HD] * r
            return carry

        lax.fori_loop(lo, hi, body, 0, unroll=2)

    for g in range(FG):
        fwd(g, 0, FH // 2)
        if g + 1 < FG:
            late(g + 1)
        fwd(g, FH // 2, FH)
        if g + 1 < FG:
            qkv(g + 1)

    attn = ot[...].T.astype(BF16)
    aw[...] = attn.reshape(aw.shape)
    o_copies = [
        remote(
            aw.at[2 * a + b],
            ah.at[pl.ds(HALF * (1 - a), HALF), core if b else 1 - core],
            (gxi(a), gyi(side) if b else y),
        )
        for a, b in quarters
    ]
    go(o_copies)
    own_a = local(aw.at[0], ah.at[pl.ds(HALF, HALF), 1 - core])
    res = dot(attn, projb[...], 1, 0).astype(BF16)
    back = dot(res, projb[...], 1, 1)
    for c in t_copies:
        c.wait_recv()
    own_t.wait()
    tw = tpw[...].reshape(n_tok, -1).astype(F32)
    dot_t[...] = ((back - tw) * loss_scale).T.astype(BF16)

    def bwd(h0, n, dq=None, dk=None, dv=None):
        g, t0 = h0 // FH, h0 % FH

        def body(i, carry):
            q, k, v = [load_qkv(part, g, t0 + i) for part in range(3)]
            h = h0 + i
            eb = ebuf[h]
            do = dot_t[rows_of(h), :].astype(F32) * rinv[h]
            dob = do.astype(BF16)
            if dq is not None:
                rd = jnp.sum(do * ot[rows_of(h), :], 0, keepdims=True)
                dp = dot(v, dob, 0, 0)
                ds = (eb.astype(F32) * (dp - rd)).astype(BF16)
                dgrp[rows_of(i, dq), :] = (dot(k, ds, 1, 0) * scale).astype(BF16)
                dgrp[rows_of(i, dk), :] = (dot(q, ds, 1, 1) * scale).astype(BF16)
            if dv is not None:
                dgrp[rows_of(i, dv), :] = dot(dob, eb, 1, 1).astype(BF16)
            return carry

        lax.fori_loop(0, n, body, 0, unroll=n)

    st = {}
    early = len(sent)

    def stage_a(i):
        snd1, rcv1 = bufs[i][:2]
        gw = width(GROUPS[i])
        dw = dot(xt[...], dgrp[:gw, :], 1, 1)
        dw = dw.reshape(ny, 2, snd1.shape[2], gw).astype(BF16)
        for cc in range(2):
            snd1[cc] = dw[:, cc]
        st["a", i] = [remote(snd1.at[1 - core], rcv1, (sib, y))]
        go(st["a", i])

    def stage_b(i):
        snd1, rcv1, s1, rcv2 = bufs[i][:4]
        for c in st["a", i]:
            c.wait_recv()
        s1[...] = (snd1[core].astype(F32) + rcv1[...].astype(F32)).astype(BF16)
        st["b", i] = [remote(s1.at[gyi(d)], rcv2.at[d - 1], (x, gyi(d))) for d in range(1, ny)]
        go(st["b", i])

    def stage_c(i):
        s1, rcv2, snd3, rcv3 = bufs[i][2:6]
        acc = s1[y].astype(F32)
        for d in range(1, ny):
            st["b", i][d - 1].wait_recv()
            acc = acc + rcv2[d - 1].astype(F32)
        snd3[...] = acc.reshape(snd3.shape).astype(BF16)
        copies = []
        for d in range(1, nz):
            piece = lax.rem(z + d, nz) if spread[i] else 0
            copies.append(remote(snd3.at[piece], rcv3.at[d - 1], (gxi(2 * d), y)))
        st["c", i] = copies
        go(copies)

    def stage_d(i):
        snd3, rcv3, fin = bufs[i][4:]
        piece = z if spread[i] else 0
        acc = snd3[piece].astype(F32)
        for d in range(1, nz):
            st["c", i][d - 1].wait_recv()
            acc = acc + rcv3[d - 1].astype(F32)
        fin[core, piece] = acc.astype(BF16)
        st["d", i] = []
        if spread[i]:
            mine = fin.at[core, z]
            st["d", i] = [remote(mine, mine, (gxi(2 * d), y)) for d in range(1, nz)]
            go(st["d", i])

    def stage_e(i):
        fin = bufs[i][6]
        for c in st["d", i]:
            c.wait_recv()
        st["e", i] = [remote(fin.at[core], fin.at[core], (sib, y))]
        go(st["e", i])

    def stage_f(i):
        for c in st["e", i]:
            c.wait_recv()
        res = flat_rows(bufs[i][6][...])
        at = 0
        for part, h0, n in GROUPS[i]:
            lo = part * INNER + h0 * HD
            grad[:, lo:lo + n * HD] = res[:, at:at + n * HD]
            at += n * HD

    def values(h0, at):
        bwd(h0, 4, None, None, at)

    bwd(0, 4, 0, FC, 2 * FC)
    stage_a(0)
    bwd(4, 2, 0, FC, 2 * FC)
    stage_b(0)
    bwd(6, 2, 2 * HD, FC + 2 * HD, 2 * FC + 2 * HD)
    stage_a(1)
    bwd(8, 2, 0, FC, 2 * FC)
    stage_b(1)
    bwd(10, 2, 2 * HD, FC + 2 * HD, 2 * FC + 2 * HD)
    stage_a(2)
    stage_c(0)
    stage_b(2)
    for c in o_copies:
        c.wait_recv()
    own_a.wait()
    outv[...] = dot(ah[...].reshape(n_tok, -1), projb[...], 1, 0).astype(BF16)
    put = local(outv, out)
    for c in sent[:early]:
        c.wait_send()
    stage_c(1)
    stage_d(0)
    stage_d(1)
    stage_c(2)
    stage_e(0)
    stage_e(1)
    stage_d(2)
    stage_f(0)
    stage_f(1)
    stage_e(2)
    stage_f(2)
    put.wait()
    for c in sent[early:]:
        c.wait_send()


def finish(b_in, g_in, b_out, g_out):
    b_out[...] = b_in[...]
    g_out[...] = g_in[...].astype(F32)


def shards(nx, ny, tokens, target, norm_gain, qkv_weight, proj_weight):
    ex, ey, ez, ch = tokens.shape
    rows = HALF * ez
    wr = qkv_weight.shape[0]
    pr = proj_weight.shape[0]
    wsplit = 4 if wr % 64 == 0 else 2
    psplit = 2 if pr % 32 == 0 else 1
    zc = 2 if wsplit == 4 else 1
    hr = wr // 2
    nz = nx // 2
    spread = [hr % (8 * nz) == 0 and on for on in SPREAD]
    n_tok = ex * ey * ez
    inner3 = qkv_weight.shape[1]
    loss_scale = 2.0 / math.sqrt(n_tok * nx * ny)
    ncopies = 9 + (FG + 1) * max(12, 2 * (ny - 1))
    ncopies += sum(2 + (ny - 1) + (nz - 1) * (2 if on else 1) for on in spread)
    any_spec = pl.BlockSpec(memory_space=pl.ANY)
    vm_spec = pl.BlockSpec(memory_space=pltpu.VMEM)
    group_bufs = []
    for group, on in zip(GROUPS, spread):
        gw = width(group)
        pieces = nz if on else 1
        prow = hr // pieces
        group_bufs += [
            pltpu.VMEM((2, ny, hr, gw), BF16),
            pltpu.VMEM((ny, hr, gw), BF16),
            pltpu.VMEM((ny, hr, gw), BF16),
            pltpu.VMEM((ny - 1, hr, gw), BF16),
            pltpu.VMEM((pieces, prow, gw), BF16),
            pltpu.VMEM((nz - 1, prow, gw), BF16),
            pltpu.VMEM((2, pieces, prow, gw), BF16),
        ]
    block, grad = pl.pallas_call(
        functools.partial(kernel, nx, ny, spread, wsplit, psplit, loss_scale),
        out_shape=(
            jax.ShapeDtypeStruct((n_tok, ch), BF16),
            jax.ShapeDtypeStruct((wr, inner3), BF16),
        ),
        in_specs=[any_spec] * 5,
        out_specs=(any_spec, vm_spec),
        scratch_shapes=[
            pltpu.VMEM((4, HALF, rows, ch), BF16),
            pltpu.VMEM((ex, 2, rows, ch), BF16),
            pltpu.VMEM((ex, 2, rows, INNER), BF16),
            pltpu.VMEM((4, HALF, rows, INNER), BF16),
            pltpu.VMEM((4, HALF, rows, INNER), BF16),
            pltpu.VMEM((ex, 2, rows, INNER), BF16),
            pltpu.VMEM((FG, ny, wsplit, wr // wsplit, 3 * FC), BF16),
            pltpu.VMEM((ny, psplit, zc, pr // psplit, ch // zc), BF16),
            pltpu.VMEM((INNER, ch), BF16),
            pltpu.VMEM((ch, n_tok), BF16),
            pltpu.VMEM((inner3, n_tok), BF16),
            pltpu.VMEM((HEADS, n_tok, n_tok), BF16),
            pltpu.VMEM((HEADS, 1, n_tok), F32),
            pltpu.VMEM((INNER, n_tok), F32),
            pltpu.VMEM((INNER, n_tok), BF16),
            pltpu.VMEM((3 * FC, n_tok), BF16),
            pltpu.VMEM((n_tok, ch), BF16),
            pltpu.VMEM((ch,), F32),
            *group_bufs,
            pltpu.SemaphoreType.DMA((ncopies,)),
            pltpu.SemaphoreType.DMA((ncopies,)),
            pltpu.SemaphoreType.DMA((3 * FG + 8,)),
        ],
        compiler_params=pltpu.CompilerParams(
            collective_id=0, has_side_effects=True, vmem_limit_bytes=60 * 2**20
        ),
        name="step",
    )(
        tokens.reshape(ex, 2, rows, ch),
        target.reshape(ex, 2, rows, ch),
        norm_gain,
        qkv_weight.reshape(wsplit, wr // wsplit, inner3),
        proj_weight.reshape(psplit, pr // psplit, ch),
    )
    steps = 2 if wr % 64 == 0 else 1
    bspec = pl.BlockSpec((n_tok // steps, ch), lambda i: (i, 0))
    gspec = pl.BlockSpec((wr // steps, inner3), lambda i: (i, 0))
    block, grad = pl.pallas_call(
        finish,
        grid=(steps,),
        out_shape=(
            jax.ShapeDtypeStruct(block.shape, BF16),
            jax.ShapeDtypeStruct(grad.shape, F32),
        ),
        in_specs=[bspec, gspec],
        out_specs=(bspec, gspec),
        name="finish",
    )(block, grad)
    return block.reshape(ex, ey, ez, ch), grad


def solution(mesh):
    nx, ny = mesh.shape["gx"], mesh.shape["gy"]
    in_specs = (
        P("gx", "gy", None, None),
        P("gx", "gy", None, None),
        P(),
        P("gy", None),
        P("gy", None),
    )
    out_specs = (P("gx", "gy", None, None), P("gy", None))
    return jax.shard_map(
        functools.partial(shards, nx, ny),
        mesh=mesh, in_specs=in_specs, out_specs=out_specs, check_vma=False,
    )
```
